512 devices in a mesh: ctx: 16 (over y, x), head: 32 (over z, core).
Axes of the slice: x: 4, y: 4, z: 16, core: 2. Of those that a mesh axis runs over, the one named last changes fastest.
Arguments:
- doc_lengths: int32 [4], replicated, may hold values from 1 to 6144, 8192 in all
- lin_q: bfloat16 [8192, 8192], P('ctx', 'head'), may hold values from -6 to 6
- lin_k: bfloat16 [8192, 8192], P('ctx', 'head'), may hold values from -6 to 6
- lin_v: bfloat16 [8192, 8192], P('ctx', 'head'), may hold values from -40 to 40
- log_decay: float32 [64, 8192], P('head', 'ctx'), may hold values from -1 to 0
- lin_gain: float32 [8192], P('head'), may hold values from 0.5 to 1.5
- soft_q: bfloat16 [8192, 8192], P('ctx', 'head'), may hold values from -48 to 48
- soft_k: bfloat16 [8192, 1024], P('ctx', 'head'), may hold values from -6 to 6
- soft_v: bfloat16 [8192, 1024], P('ctx', 'head'), may hold values from -6 to 6
Outputs:
- lin_out: bfloat16 [8192, 8192], P('ctx', 'head')
- soft_out: bfloat16 [8192, 8192], P('ctx', 'head')
The draws below stay inside these ranges and needn't reach their ends.
Inputs may be any that keep to these rules, and one draw needn't show every extreme that they name: `doc_lengths`: the 4 lengths sum to 8192 and the largest is exactly 6144.
All inputs are finite; a program needn't handle non-finite values.
Results may differ from the reference program's by a relative error of at most 0.015.
Values may be sent and summed in bfloat16 or wider, within the bound.
A program may use at most 64 MiB of HBM per device.

```python
import math
import jax
import jax.numpy as jnp
import numpy as np
from jax import lax

QUERY_HEAD_COUNT = 64
KVH = 8
DH = 128
BLK = 256
DOCS = 4
TOK_DEV = 512
WINDOW_TOKENS = 8192
MOST = 6144


def draw_lin_v(key, part):
    first, second, third = jax.random.split(key, 3)
    columns = QUERY_HEAD_COUNT * DH
    base = jnp.clip(jax.random.normal(first, (WINDOW_TOKENS, columns)), -4.0, 4.0)
    row_scale = 10.0 ** jax.random.uniform(second, (WINDOW_TOKENS, 1))
    column_scale = 10.0 ** jax.random.uniform(third, (1, columns))
    return (base * row_scale * column_scale / 10.0).astype(jnp.bfloat16)


def draw_log_decay(key, part):
    option_key, quick_key, gradual_key, multiplier_key, spike_key, magnitude_key, region_key, region_rate_key = jax.random.split(key, 8)
    regions = WINDOW_TOKENS // TOK_DEV
    mixed = jax.random.randint(option_key, (QUERY_HEAD_COUNT, 1), 0, 2) == 0
    decay_factor = jnp.exp(jax.random.uniform(multiplier_key, (QUERY_HEAD_COUNT, WINDOW_TOKENS), minval=math.log(0.5), maxval=math.log(2.0)))
    fast_rate = jnp.exp(jax.random.uniform(quick_key, (QUERY_HEAD_COUNT, 1), minval=math.log(1.0 / 50.0), maxval=math.log(1.0 / 30.0)))
    slow_rate = jax.random.uniform(gradual_key, (QUERY_HEAD_COUNT, 1), minval=0.1, maxval=0.4) * (math.log(10.0) / WINDOW_TOKENS)
    region_fast = jax.random.randint(region_key, (QUERY_HEAD_COUNT, regions), 0, 2) == 0
    region_medium = jnp.exp(jax.random.uniform(region_rate_key, (QUERY_HEAD_COUNT, regions), minval=math.log(1.0 / 4000.0), maxval=math.log(1.0 / 400.0)))
    region_rate = jnp.where(region_fast, fast_rate, region_medium)
    region_rate = jnp.repeat(region_rate, TOK_DEV, axis=1)
    decay_rate = jnp.where(mixed, region_rate, slow_rate)
    outlier_flags = (jax.random.randint(spike_key, (QUERY_HEAD_COUNT, WINDOW_TOKENS), 0, WINDOW_TOKENS) < 2).astype(jnp.float32)
    outlier_magnitude = jax.random.uniform(magnitude_key, (QUERY_HEAD_COUNT, WINDOW_TOKENS), minval=0.22, maxval=0.69)
    return (-(decay_rate * decay_factor) - outlier_flags * outlier_magnitude).astype(jnp.float32)


def paired_soft(key):
    base_key = jax.random.fold_in(key, 7)
    query_key = jax.random.fold_in(base_key, 0)
    keys_key = jax.random.fold_in(base_key, 1)
    loud_key = jax.random.fold_in(base_key, 4)
    loud = jax.random.randint(loud_key, (WINDOW_TOKENS,), 0, 64) == 0
    queries = jnp.clip(jax.random.normal(query_key, (WINDOW_TOKENS, QUERY_HEAD_COUNT * DH)), -4.0, 4.0)
    loud_rows = jnp.sign(queries) * (30.0 + 4.0 * jnp.abs(queries))
    queries = jnp.where(loud[:, None], loud_rows, queries)
    keys_all = jnp.clip(jax.random.normal(keys_key, (WINDOW_TOKENS, KVH * DH)), -4.0, 4.0)
    return (queries.astype(jnp.float32), keys_all.astype(jnp.float32))


def draw_soft_q(key, part):
    return paired_soft(key)[0].astype(jnp.bfloat16)


def draw_soft_k(key, part):
    return paired_soft(key)[1].astype(jnp.bfloat16)


def level_of(key, extent, pieces, smallest, high):
    def one(axis_at, blocks):
        draws = jax.random.uniform(jax.random.fold_in(jax.random.fold_in(key, 6), axis_at), (blocks,), jnp.float32, smallest / len(pieces), high / len(pieces))
        return jnp.repeat(jnp.exp(draws), extent[axis_at] // blocks).reshape((-1,) + (1,) * (len(extent) - axis_at - 1))

    level = one(*pieces[0])
    for cut in pieces[1:]:
        level = level * one(*cut)
    return level


def split_up(number_of, total, bound, lean):
    portions = [(1 << 20) // math.isqrt(rank ** lean) + 1 for rank in range(2, number_of + 1)]
    rest, given = total - bound - (number_of - 1), [1] * (number_of - 1)
    while rest > 0:
        free = [i for i in range(number_of - 1) if given[i] < bound]
        pool, remaining = sum([portions[i] for i in free]), rest
        for i in free:
            addition = min(bound - given[i], max(1, remaining * portions[i] // pool), rest)
            given[i] = given[i] + addition
            rest = rest - addition
    return np.array([bound] + given)


def uneven(key, amount, total, bound, lean):
    if amount == 2:
        one = jax.random.randint(key, (), max(1, total - bound), min(bound, total - 1) + 1)
        return jnp.stack([one, total - one])
    tallies = jnp.asarray(split_up(amount, total, bound, lean), jnp.int32)
    twos = (amount - 1) // 2
    source_of, sink = tallies[1:1 + 2 * twos:2], tallies[2:2 + 2 * twos:2]
    room = jnp.minimum(source_of - 1, bound - sink)
    passed = jax.random.randint(jax.random.fold_in(key, 1), (twos,), 0, 1 << 20) % (room + 1)
    tallies = tallies.at[1:1 + 2 * twos:2].set(source_of - passed).at[2:2 + 2 * twos:2].set(sink + passed)
    return tallies[jax.random.permutation(jax.random.fold_in(key, 2), amount)]


def centred(own_key, shape, width, bound, cuts=(), kind=jnp.bfloat16):
    gain = level_of(own_key, shape, cuts, -0.22, 0.18) if cuts else 1.0
    entries = jax.random.normal(own_key, shape, jnp.float32) * width * gain
    return jnp.minimum(jnp.maximum(entries, -bound), bound).astype(kind)


def setup_inputs(seed: int = 0) -> dict:
    streams_of = jax.random.split(jax.random.key(seed), 10)
    doc_lengths = uneven(streams_of[0], DOCS, WINDOW_TOKENS, MOST, 2).astype(jnp.int32)
    lin_q = centred(streams_of[1], (WINDOW_TOKENS, QUERY_HEAD_COUNT * DH), 1.0, 6.0, ((0, 16), (1, 32)))
    lin_k = centred(streams_of[2], (WINDOW_TOKENS, QUERY_HEAD_COUNT * DH), 1.0, 6.0, ((0, 16), (1, 32)))
    lin_v = draw_lin_v(jax.random.fold_in(streams_of[9], 71), 0)
    log_decay = draw_log_decay(jax.random.fold_in(streams_of[9], 71), 0)
    lin_gain = jnp.clip(1.0 + 0.1 * jax.random.normal(streams_of[5], (QUERY_HEAD_COUNT * DH,), jnp.float32), 0.5, 1.5)
    soft_q = draw_soft_q(jax.random.fold_in(streams_of[9], 71), 0)
    soft_k = draw_soft_k(jax.random.fold_in(streams_of[9], 71), 0)
    soft_v = centred(streams_of[8], (WINDOW_TOKENS, KVH * DH), 1.0, 6.0, ((0, 16), (1, 32)))
    return {"doc_lengths": doc_lengths, "lin_q": lin_q, "lin_k": lin_k, "lin_v": lin_v, "log_decay": log_decay, "lin_gain": lin_gain, "soft_q": soft_q, "soft_k": soft_k, "soft_v": soft_v}


def doc_index(doc_lengths, positions):
    bounds = jnp.cumsum(doc_lengths).astype(jnp.int32)
    counted = lax.optimization_barrier(jnp.sum((bounds[None, :] <= positions[:, None]).astype(jnp.int32), axis=1)).astype(jnp.int32)
    return jnp.where(positions < 0, -1, counted).astype(jnp.int32)

def lightning_block(carry_state, scan_items):
    queries, keys_block, values_block, decay_block, segs_block, seg_before = scan_items
    running = jnp.cumsum(decay_block, axis=1)
    block_len = segs_block.shape[0]
    rows_iota = lax.broadcasted_iota(jnp.int32, (block_len, block_len), 0)
    cols_iota = lax.broadcasted_iota(jnp.int32, (block_len, block_len), 1)
    allowed = (rows_iota >= cols_iota) & (segs_block[:, None] == segs_block[None, :])
    spread = jnp.where(allowed[None], running[:, :, None] - running[:, None, :], 0.0)
    decays = jnp.where(allowed[None], jnp.exp(spread), 0.0)
    query_wide = queries.astype(jnp.float32)
    key_wide = keys_block.astype(jnp.float32)
    value_wide = values_block.astype(jnp.float32)
    scores = jnp.einsum('ihd,jhd->hij', query_wide, key_wide, precision=lax.Precision.HIGHEST) * decays
    scores = lax.optimization_barrier(scores.astype(jnp.bfloat16)).astype(jnp.float32)
    inside = jnp.einsum('hij,jhd->ihd', scores, value_wide, precision=lax.Precision.HIGHEST)
    carried = (segs_block == seg_before).astype(jnp.float32)
    entering = jnp.exp(running) * carried[None, :]
    state_low = lax.optimization_barrier(carry_state.astype(jnp.bfloat16)).astype(jnp.float32)
    across = jnp.einsum('ihd,hde->ihe', query_wide, state_low, precision=lax.Precision.HIGHEST)
    across = across * entering.T[:, :, None]
    closing = running[:, -1:]
    tail_mask = (segs_block == segs_block[-1]).astype(jnp.float32)
    weights = jnp.exp(closing - running) * tail_mask[None, :]
    weighted = key_wide * weights.T[:, :, None]
    weighted = lax.optimization_barrier(weighted.astype(jnp.bfloat16)).astype(jnp.float32)
    update = jnp.einsum('jhd,jhe->hde', weighted, value_wide, precision=lax.Precision.HIGHEST)
    kept_flag = (segs_block[-1] == seg_before).astype(jnp.float32)
    decay_factor = kept_flag * jnp.exp(closing[:, 0])
    new_state = decay_factor[:, None, None] * carry_state + update
    return (new_state, inside + across)

def lightning(lin_q, lin_k, lin_v, log_decay, lin_gain, doc_ids):
    blocks = WINDOW_TOKENS // BLK
    shaped = (blocks, BLK, QUERY_HEAD_COUNT, DH)
    query_blocks = lin_q.reshape(shaped)
    key_blocks = lin_k.reshape(shaped)
    value_blocks = lin_v.reshape(shaped)
    decay_blocks = log_decay.reshape(QUERY_HEAD_COUNT, blocks, BLK).transpose(1, 0, 2)
    seg_blocks = doc_ids.reshape(blocks, BLK)
    befores = jnp.concatenate([jnp.full((1,), -1, jnp.int32), seg_blocks[:-1, -1].astype(jnp.int32)])
    start_state = jnp.zeros((QUERY_HEAD_COUNT, DH, DH), jnp.float32)
    _, outputs = lax.scan(lightning_block, start_state, (query_blocks, key_blocks, value_blocks, decay_blocks, seg_blocks, befores))
    raw_out = outputs.reshape(WINDOW_TOKENS, QUERY_HEAD_COUNT, DH)
    norm_scale = lax.rsqrt(lax.optimization_barrier(jnp.mean(raw_out * raw_out, axis=2, keepdims=True)) + 1e-06)
    normed = raw_out * norm_scale * lin_gain.reshape(1, QUERY_HEAD_COUNT, DH)
    return normed.reshape(WINDOW_TOKENS, QUERY_HEAD_COUNT * DH).astype(jnp.bfloat16)

def softmax_head(head_query, head_keys, head_values, doc_ids):
    scores = jnp.dot(head_query, head_keys.T, preferred_element_type=jnp.float32) * DH ** (-0.5)
    positions = jnp.arange(WINDOW_TOKENS, dtype=jnp.int32)
    allowed = (positions[None, :] <= positions[:, None]) & (doc_ids[None, :] == doc_ids[:, None])
    masked = jnp.where(allowed, scores, -jnp.inf)
    row_top = lax.optimization_barrier(jnp.max(masked, axis=1, keepdims=True))
    exp_terms = jnp.where(allowed, jnp.exp(scores - row_top), 0.0)
    row_total = lax.optimization_barrier(jnp.sum(exp_terms, axis=1, keepdims=True))
    weights = exp_terms.astype(jnp.bfloat16)
    return jnp.dot(weights, head_values, preferred_element_type=jnp.float32) / row_total

def reference(doc_lengths, lin_q, lin_k, lin_v, log_decay, lin_gain, soft_q, soft_k, soft_v):
    positions = jnp.arange(WINDOW_TOKENS, dtype=jnp.int32)
    doc_ids = doc_index(doc_lengths, positions)
    lin_out = lightning(lin_q, lin_k, lin_v, log_decay, lin_gain, doc_ids)
    group_size = QUERY_HEAD_COUNT // KVH
    query_heads = soft_q.reshape(WINDOW_TOKENS, QUERY_HEAD_COUNT, DH).transpose(1, 0, 2)
    key_heads = jnp.repeat(soft_k.reshape(WINDOW_TOKENS, KVH, DH).transpose(1, 0, 2), group_size, axis=0)
    value_heads = jnp.repeat(soft_v.reshape(WINDOW_TOKENS, KVH, DH).transpose(1, 0, 2), group_size, axis=0)

    def one_head(head_items):
        return softmax_head(head_items[0], head_items[1], head_items[2], doc_ids)
    attended = lax.map(one_head, (query_heads, key_heads, value_heads))
    soft_out = attended.transpose(1, 0, 2).reshape(WINDOW_TOKENS, QUERY_HEAD_COUNT * DH).astype(jnp.bfloat16)
    return (lin_out, soft_out)
```

```python
import math

import jax
import jax.numpy as jnp
from jax import lax
from jax.experimental import pallas as pl
from jax.experimental.pallas import tpu as pltpu
from jax.sharding import PartitionSpec as P

DH = 128
BLK = 256
TOK = 512
REACH = 12
HALF = 256
BIG = 1048576.0
SCALE = math.log2(math.e) / math.sqrt(DH)
MESH = pl.DeviceIdType.MESH
F32 = jnp.float32
BF16 = jnp.bfloat16
AB = (((1,), (0,)), ((), ()))
ABT = (((1,), (1,)), ((), ()))
ATB = (((0,), (0,)), ((), ()))


def mm(a, b, dims=AB):
    return lax.dot_general(a, b, dims, preferred_element_type=F32)


def kernel(
    doc, lq_in, lk_in, lv_in, ld_in, gain_in, sq_in, sk_in, sv_in,
    lin_out, soft_out,
    lq, lk, lv, ld, gain, sq,
    kv, qx, top, acc, raw, cum, row_st, col_st, first_up, carry,
    in_sem, x_send, x_recv, s_send, s_recv, z_send, z_recv, t_send, t_recv,
    r_send, r_recv, c_send, c_recv,
):
    me = lax.axis_index("ctx")
    hd = lax.axis_index("head")
    col, line = lax.rem(me, 4), me // 4
    sib = hd + 1 - 2 * lax.rem(hd, 2)
    zp = hd + 2 - 4 * lax.rem(hd // 2, 2)
    quarter = lax.rem(hd, 4)
    zquarter = lax.rem(zp, 4)
    n_lo = jnp.minimum(me, REACH)
    n_hi = jnp.minimum(15 - me, REACH)

    loads = [
        pltpu.make_async_copy(a, b, in_sem.at[i])
        for i, (a, b) in enumerate(
            [(sk_in, kv.at[0, quarter, :32]), (sv_in, kv.at[0, quarter, 32:]), (sq_in, sq), (lq_in, lq), (lk_in, lk), (lv_in, lv), (ld_in, ld), (gain_in, gain)]
        )
    ]
    for load in loads:
        load.start()

    barrier = pltpu.get_barrier_semaphore()

    def greet(ctx, head):
        pl.semaphore_signal(barrier, inc=1, device_id=(ctx, head), device_id_type=MESH)

    greet(me, sib)
    greet(me, zp)
    lax.fori_loop(1, n_lo + 1, lambda d, c: (greet(me - d, hd), c)[1], 0)
    lax.fori_loop(1, n_hi + 1, lambda d, c: (greet(me + d, hd), c)[1], 0)

    loads[0].wait()
    loads[1].wait()
    pl.semaphore_wait(barrier, 2 + n_lo + n_hi)

    def copy(src, dst, send, recv, ctx, head):
        return pltpu.make_async_remote_copy(
            src_ref=src, dst_ref=dst, send_sem=send, recv_sem=recv, device_id=(ctx, head), device_id_type=MESH
        )

    def x_copy(d):
        return copy(kv.at[0, quarter], kv.at[d, quarter], x_send.at[d], x_recv.at[d], me + d, hd)

    def s_copy(d):
        return copy(kv.at[d, quarter], kv.at[d, quarter], s_send.at[d], s_recv.at[d], me, sib)

    def z_copy(d):
        return copy(kv.at[d, quarter], kv.at[d, quarter], z_send.at[d], z_recv.at[d], me, zp)

    def t_copy(d):
        return copy(kv.at[d, zquarter], kv.at[d, zquarter], t_send.at[d], t_recv.at[d], me, sib)

    def r_copy(k):
        return copy(row_st.at[0], row_st.at[k], r_send.at[k], r_recv.at[k], line * 4 + lax.rem(col + k, 4), hd)

    def c_copy(k):
        return copy(col_st.at[0], col_st.at[k], c_send.at[k], c_recv.at[k], me + 4 * k, hd)

    def pass_own(d):
        @pl.when(d <= n_lo)
        def _():
            x_copy(d).wait_recv()
            s_copy(d).start()
            z_copy(d).start()

    def pass_far(d):
        @pl.when(d <= n_lo)
        def _():
            z_copy(d).wait_recv()
            t_copy(d).start()

    s_copy(0).start()
    z_copy(0).start()
    lax.fori_loop(1, n_hi + 1, lambda d, c: (x_copy(d).start(), c)[1], 0)

    bounds = [doc[0], doc[0] + doc[1], doc[0] + doc[1] + doc[2]]

    def doc_start(p):
        start = jnp.zeros_like(p)
        for b in bounds:
            start = jnp.maximum(start, jnp.where(b <= p, b, 0))
        return start

    def doc_id(p):
        count = jnp.zeros_like(p)
        for b in bounds:
            count = count + jnp.where(b <= p, 1, 0)
        return count

    base = me * TOK

    loads[2].wait()
    rows = base + lax.broadcasted_iota(jnp.int32, (TOK, DH), 0)
    lanes = lax.broadcasted_iota(jnp.int32, (TOK, DH), 1)
    marks = jnp.where(doc_id(rows) == lanes, 1.0, 0.0).astype(BF16)
    for h in range(2):
        qx[h * TOK : (h + 1) * TOK, :DH] = sq[:, h * DH : (h + 1) * DH]
        qx[h * TOK : (h + 1) * TOK, DH:] = marks

    for load in loads[3:]:
        load.wait()
    tri = jnp.where(
        lax.broadcasted_iota(jnp.int32, (BLK, BLK), 0) <= lax.broadcasted_iota(jnp.int32, (BLK, BLK), 1), 1.0, 0.0
    ).astype(F32)
    steps = jnp.concatenate([ld[:, :BLK], ld[:, BLK:], jnp.zeros((4, BLK), F32)], axis=0)
    running = lax.dot_general(steps, tri, AB, precision=lax.Precision.HIGHEST, preferred_element_type=F32)
    cum[...] = running.T
    row_of = lax.broadcasted_iota(jnp.int32, (BLK, BLK), 0)
    col_of = lax.broadcasted_iota(jnp.int32, (BLK, BLK), 1)
    col_pos = lax.broadcasted_iota(jnp.int32, (BLK, 1), 0)

    def parts(b, h):
        r = slice(b * BLK, (b + 1) * BLK)
        c = slice(h * DH, (h + 1) * DH)
        return r, c, running[2 * b + h : 2 * b + h + 1, :], cum[:, 2 * b + h : 2 * b + h + 1]

    def through(b, h):
        end = running[2 * b + h : 2 * b + h + 1, BLK - 1 :]
        return jnp.exp(end)

    def kept(first, last):
        return jnp.where(doc_start(last) <= first - 1, 1.0, 0.0).astype(F32)

    for h in range(2):
        ups = []
        for b in range(2):
            r, c, across_row, down_col = parts(b, h)
            first = base + b * BLK
            start = doc_start(first + col_pos) - first
            allowed = (col_of <= row_of) & (col_of >= start)
            decays = jnp.exp(down_col - across_row)
            a = jnp.where(allowed, mm(lq[r, c], lk[r, c], ABT) * decays, 0.0).astype(BF16)
            raw[r, c] = mm(a, lv[r, c])
            tail = jnp.where(
                first + col_pos >= doc_start(first + BLK - 1), jnp.exp(across_row[:, BLK - 1 :] - down_col), 0.0
            )
            w = (lk[r, c].astype(F32) * tail).astype(BF16)
            ups.append(mm(w, lv[r, c], ATB))
        first_up[h] = ups[0]
        whole = kept(base + BLK, base + TOK - 1) * through(1, h) * ups[0] + ups[1]
        row_st[0, h * DH : (h + 1) * DH] = whole.astype(BF16)
    pad_row = lax.broadcasted_iota(jnp.int32, (16, DH), 0)

    def factor_rows(f0, f1):
        hi0, hi1 = f0.astype(BF16).astype(F32), f1.astype(BF16).astype(F32)
        out = jnp.where(pad_row == 0, hi0, 0.0)
        out = jnp.where(pad_row == 1, f0 - hi0, out)
        out = jnp.where(pad_row == 2, hi1, out)
        return jnp.where(pad_row == 3, f1 - hi1, out).astype(BF16)

    row_st[0, 2 * DH :] = factor_rows(through(0, 0) * through(1, 0), through(0, 1) * through(1, 1))
    for k in range(1, 4):
        r_copy(k).start()

    def factor_of(block, h):
        tail = block[2 * DH :].astype(F32)
        return tail[2 * h : 2 * h + 1] + tail[2 * h + 1 : 2 * h + 2]

    def keys_of(d):
        quarters = [kv[d, i, :32] for i in range(4)]
        ids = doc_id((me - d) * TOK + lax.broadcasted_iota(jnp.int32, (16, TOK), 1))
        which = lax.broadcasted_iota(jnp.int32, (16, TOK), 0)
        block = jnp.where((which < 4) & (which != ids), -BIG, 0.0).astype(BF16)
        return jnp.concatenate(quarters + [block, jnp.zeros((DH - 16, TOK), BF16)], axis=0)

    def values_of(d):
        quarters = [kv[d, i, 32:] for i in range(4)]
        return jnp.concatenate(quarters + [jnp.ones((DH, TOK), BF16)], axis=0)

    def arrived(d):
        s_copy(d).wait_recv()
        t_copy(d).wait_recv()

    def diagonal():
        keys, values = keys_of(0), values_of(0)
        for t in range(4):
            r = slice(t * HALF, (t + 1) * HALF)
            s = mm(qx[r], keys)
            pos = (t % 2) * HALF + lax.broadcasted_iota(jnp.int32, (HALF, TOK), 0)
            s = jnp.where(lax.broadcasted_iota(jnp.int32, (HALF, TOK), 1) <= pos, s, -BIG)
            m = jnp.max(s, axis=1, keepdims=True)
            p = jnp.exp2((s - m) * SCALE).astype(BF16)
            acc[r] = mm(p, values, ABT)
            top[r] = jnp.broadcast_to(m, (HALF, DH))

    def visit(d):
        keys, values = keys_of(d), values_of(d)
        for t in range(4):
            r = slice(t * HALF, (t + 1) * HALF)
            s = mm(qx[r], keys)
            old = top[r, :1]
            m = jnp.maximum(old, jnp.max(s, axis=1, keepdims=True))
            p = jnp.exp2((s - m) * SCALE).astype(BF16)
            acc[r] = jnp.exp2((old - m) * SCALE) * acc[r] + mm(p, values, ABT)
            top[r] = jnp.broadcast_to(m, (HALF, DH))

    pass_far(0)
    pass_own(1)
    arrived(0)
    diagonal()
    pass_far(1)
    pass_own(2)

    for k in range(1, 4):
        r_copy(k).wait_recv()
    line_first = line * 4 * TOK
    enter_row = []
    enter_factor = []
    for h in range(2):
        total = jnp.zeros((DH, DH), F32)
        before = jnp.zeros((DH, DH), F32)
        factor = jnp.ones((1, DH), F32)
        factor_before = jnp.ones((1, DH), F32)
        plain = jnp.ones((1, DH), F32)
        for x in range(4):
            block = row_st[lax.rem(col - x + 4, 4)]
            own = col == x
            before = jnp.where(own, total, before)
            factor_before = jnp.where(own, factor, factor_before)
            f = factor_of(block, h)
            fk = f * kept(line_first + x * TOK, line_first + (x + 1) * TOK - 1)
            total = fk * total + block[h * DH : (h + 1) * DH].astype(F32)
            factor = factor * fk
            plain = plain * f
        carry[h] = before
        enter_factor.append(factor_before)
        enter_row.append(plain)
        col_st[0, h * DH : (h + 1) * DH] = total.astype(BF16)
    col_st[0, 2 * DH :] = factor_rows(enter_row[0], enter_row[1])
    n_down = 3 - line
    lax.fori_loop(1, n_down + 1, lambda k, c: (c_copy(k).start(), c)[1], 0)

    def loop_body(d, c):
        pass_far(d + 1)
        pass_own(d + 2)
        arrived(d)
        visit(d)
        return c

    early = jnp.minimum(n_lo, 2)
    lax.fori_loop(1, early + 1, loop_body, 0)

    def column(i, state):
        k = line - i
        c_copy(k).wait_recv()
        block = col_st[k]
        first = i * 4 * TOK
        keep = kept(first, first + 4 * TOK - 1)
        return tuple(
            keep * factor_of(block, h) * state[h] + block[h * DH : (h + 1) * DH].astype(F32) for h in range(2)
        )

    entered = lax.fori_loop(0, line, column, (jnp.zeros((DH, DH), F32), jnp.zeros((DH, DH), F32)))
    for h in range(2):
        state = enter_factor[h] * entered[h] + carry[h]
        for b in range(2):
            r, c, _, down_col = parts(b, h)
            first = base + b * BLK
            mine = jnp.where(doc_start(first + col_pos) <= first - 1, jnp.exp(down_col), 0.0)
            full = raw[r, c] + mine * mm(lq[r, c], state.astype(BF16))
            scale = lax.rsqrt(jnp.mean(full * full, axis=1, keepdims=True) + 1e-6)
            lin_out[r, c] = (full * scale * gain[:, c]).astype(BF16)
            if b == 0:
                state = kept(base, base + BLK - 1) * through(0, h) * state + first_up[h]

    lax.fori_loop(early + 1, n_lo + 1, loop_body, 0)

    for t in range(4):
        r = slice(t * HALF, (t + 1) * HALF)
        out = acc[r, :DH] / acc[r, DH:]
        h, b = t // 2, t % 2
        soft_out[b * HALF : (b + 1) * HALF, h * DH : (h + 1) * DH] = out.astype(BF16)

    def sent(d, c):
        s_copy(d).wait_send()
        z_copy(d).wait_send()
        t_copy(d).wait_send()
        return c

    lax.fori_loop(0, n_lo + 1, sent, 0)
    lax.fori_loop(1, n_hi + 1, lambda d, c: (x_copy(d).wait_send(), c)[1], 0)
    for k in range(1, 4):
        r_copy(k).wait_send()
    lax.fori_loop(1, n_down + 1, lambda k, c: (c_copy(k).wait_send(), c)[1], 0)


def local(doc_lengths, lin_q, lin_k, lin_v, log_decay, lin_gain, soft_q, soft_k, soft_v):
    vmem = pltpu.VMEM
    dma = pltpu.SemaphoreType.DMA
    wide = (TOK, 2 * DH)
    slots = REACH + 1
    return pl.pallas_call(
        kernel,
        out_shape=(jax.ShapeDtypeStruct(wide, BF16), jax.ShapeDtypeStruct(wide, BF16)),
        in_specs=[pl.BlockSpec(memory_space=pltpu.SMEM)] + [pl.BlockSpec(memory_space=pl.ANY)] * 8,
        out_specs=(pl.BlockSpec(memory_space=vmem), pl.BlockSpec(memory_space=vmem)),
        scratch_shapes=[
            vmem(wide, BF16), vmem(wide, BF16), vmem(wide, BF16), vmem((2, TOK), F32), vmem((1, 2 * DH), F32),
            vmem(wide, BF16),
            vmem((slots, 4, 64, TOK), BF16), vmem((2 * TOK, 2 * DH), BF16), vmem((2 * TOK, DH), F32),
            vmem((2 * TOK, 2 * DH), F32), vmem(wide, F32), vmem((BLK, 8), F32),
            vmem((4, 2 * DH + 16, DH), BF16), vmem((4, 2 * DH + 16, DH), BF16), vmem((2, DH, DH), F32),
            vmem((2, DH, DH), F32),
            dma((8,)), dma((slots,)), dma((slots,)), dma((slots,)), dma((slots,)), dma((slots,)), dma((slots,)),
            dma((slots,)), dma((slots,)), dma((4,)), dma((4,)), dma((4,)), dma((4,)),
        ],
        compiler_params=pltpu.CompilerParams(
            collective_id=0, has_side_effects=True, vmem_limit_bytes=40 * 1024 * 1024
        ),
    )(doc_lengths, lin_q, lin_k, lin_v, log_decay, lin_gain.reshape(1, 2 * DH), soft_q, soft_k.T, soft_v.T)


def solution(mesh):
    both = P("ctx", "head")
    return jax.shard_map(
        local,
        mesh=mesh,
        in_specs=(P(), both, both, both, P("head", "ctx"), P("head"), both, both, both),
        out_specs=(both, both),
        check_vma=False,
    )
```

```python
import math

import jax
import jax.numpy as jnp
from jax import lax
from jax.experimental import pallas as pl
from jax.experimental.pallas import tpu as pltpu
from jax.sharding import PartitionSpec as P

DH = 128
BLK = 256
TOK = 512
NEAR = 9
LOOK = 4
REACH = 12
HALF = 256
BIG = 1048576.0
SCALE = math.log2(math.e) / math.sqrt(DH)
MESH = pl.DeviceIdType.MESH
F32 = jnp.float32
BF16 = jnp.bfloat16
AB = (((1,), (0,)), ((), ()))
ABT = (((1,), (1,)), ((), ()))
ATB = (((0,), (0,)), ((), ()))


def mm(a, b, dims=AB):
    return lax.dot_general(a, b, dims, preferred_element_type=F32)


def kernel(
    doc, lq_in, lk_in, lv_in, ld_in, gain_in, sq_in, sk_in, sv_in,
    lin_out, soft_out,
    lq, lk, lv, ld, gain, sq,
    kv, qx, top, acc, raw, cum, row_st, col_st, first_up, carry,
    in_sem, x_send, x_recv, y_send, s_send, s_recv, z_send, z_recv, t_send, t_recv,
    r_send, r_recv, c_send, c_recv,
):
    me = lax.axis_index("ctx")
    hd = lax.axis_index("head")
    col, line = lax.rem(me, 4), me // 4
    sib = hd + 1 - 2 * lax.rem(hd, 2)
    zp = hd + 2 - 4 * lax.rem(hd // 2, 2)
    quarter = lax.rem(hd, 4)
    zquarter = lax.rem(zp, 4)
    n_lo = jnp.minimum(me, REACH)
    n_hi = jnp.minimum(15 - me, REACH)

    loads = [
        pltpu.make_async_copy(a, b, in_sem.at[i])
        for i, (a, b) in enumerate(
            [(sk_in, kv.at[0, quarter, :32]), (sv_in, kv.at[0, quarter, 32:]), (sq_in, sq), (lq_in, lq), (lk_in, lk), (lv_in, lv), (ld_in, ld), (gain_in, gain)]
        )
    ]
    for load in loads:
        load.start()

    barrier = pltpu.get_barrier_semaphore()

    def greet(ctx, head):
        pl.semaphore_signal(barrier, inc=1, device_id=(ctx, head), device_id_type=MESH)

    greet(me, sib)
    greet(me, zp)
    lax.fori_loop(1, n_lo + 1, lambda d, c: (greet(me - d, hd), c)[1], 0)
    lax.fori_loop(1, n_hi + 1, lambda d, c: (greet(me + d, hd), c)[1], 0)

    loads[0].wait()
    loads[1].wait()
    pl.semaphore_wait(barrier, 2 + n_lo + n_hi)

    def copy(src, dst, send, recv, ctx, head):
        return pltpu.make_async_remote_copy(
            src_ref=src, dst_ref=dst, send_sem=send, recv_sem=recv, device_id=(ctx, head), device_id_type=MESH
        )

    def x_copy(d):
        return copy(kv.at[0, quarter], kv.at[d, quarter], x_send.at[d], x_recv.at[d], me + d, hd)

    def y_copy(d):
        return copy(kv.at[0, zquarter], kv.at[d, zquarter], y_send.at[d], z_recv.at[d], me + d, hd)

    def s_copy(d):
        return copy(kv.at[d, quarter], kv.at[d, quarter], s_send.at[d], s_recv.at[d], me, sib)

    def z_copy(d):
        return copy(kv.at[d, quarter], kv.at[d, quarter], z_send.at[d], z_recv.at[d], me, zp)

    def t_copy(d):
        return copy(kv.at[d, zquarter], kv.at[d, zquarter], t_send.at[d], t_recv.at[d], me, sib)

    def r_copy(k):
        return copy(row_st.at[0], row_st.at[k], r_send.at[k], r_recv.at[k], line * 4 + lax.rem(col + k, 4), hd)

    def c_copy(k):
        return copy(col_st.at[0], col_st.at[k], c_send.at[k], c_recv.at[k], me + 4 * k, hd)

    def pass_own(d):
        @pl.when(d <= n_lo)
        def _():
            x_copy(d).wait_recv()
            s_copy(d).start()
            pl.when(d <= NEAR)(lambda: z_copy(d).start())

    def pass_far(d):
        @pl.when(d <= n_lo)
        def _():
            z_copy(d).wait_recv()
            t_copy(d).start()

    s_copy(0).start()
    z_copy(0).start()
    lax.fori_loop(1, n_hi + 1, lambda d, c: (x_copy(d).start(), c)[1], 0)

    bounds = [doc[0], doc[0] + doc[1], doc[0] + doc[1] + doc[2]]

    def doc_start(p):
        start = jnp.zeros_like(p)
        for b in bounds:
            start = jnp.maximum(start, jnp.where(b <= p, b, 0))
        return start

    def doc_id(p):
        count = jnp.zeros_like(p)
        for b in bounds:
            count = count + jnp.where(b <= p, 1, 0)
        return count

    base = me * TOK

    loads[2].wait()
    rows = base + lax.broadcasted_iota(jnp.int32, (TOK, DH), 0)
    lanes = lax.broadcasted_iota(jnp.int32, (TOK, DH), 1)
    marks = jnp.where(doc_id(rows) == lanes, 1.0, 0.0).astype(BF16)
    for h in range(2):
        qx[h * TOK : (h + 1) * TOK, :DH] = sq[:, h * DH : (h + 1) * DH]
        qx[h * TOK : (h + 1) * TOK, DH:] = marks

    for load in loads[3:]:
        load.wait()
    tri = jnp.where(
        lax.broadcasted_iota(jnp.int32, (BLK, BLK), 0) <= lax.broadcasted_iota(jnp.int32, (BLK, BLK), 1), 1.0, 0.0
    ).astype(F32)
    steps = jnp.concatenate([ld[:, :BLK], ld[:, BLK:], jnp.zeros((4, BLK), F32)], axis=0)
    running = lax.dot_general(steps, tri, AB, precision=lax.Precision.HIGHEST, preferred_element_type=F32)
    cum[...] = running.T
    row_of = lax.broadcasted_iota(jnp.int32, (BLK, BLK), 0)
    col_of = lax.broadcasted_iota(jnp.int32, (BLK, BLK), 1)
    col_pos = lax.broadcasted_iota(jnp.int32, (BLK, 1), 0)

    def parts(b, h):
        r = slice(b * BLK, (b + 1) * BLK)
        c = slice(h * DH, (h + 1) * DH)
        return r, c, running[2 * b + h : 2 * b + h + 1, :], cum[:, 2 * b + h : 2 * b + h + 1]

    def through(b, h):
        end = running[2 * b + h : 2 * b + h + 1, BLK - 1 :]
        return jnp.exp(end)

    def kept(first, last):
        return jnp.where(doc_start(last) <= first - 1, 1.0, 0.0).astype(F32)

    for h in range(2):
        ups = []
        for b in range(2):
            r, c, across_row, down_col = parts(b, h)
            first = base + b * BLK
            start = doc_start(first + col_pos) - first
            allowed = (col_of <= row_of) & (col_of >= start)
            decays = jnp.exp(down_col - across_row)
            a = jnp.where(allowed, mm(lq[r, c], lk[r, c], ABT) * decays, 0.0).astype(BF16)
            raw[r, c] = mm(a, lv[r, c])
            tail = jnp.where(
                first + col_pos >= doc_start(first + BLK - 1), jnp.exp(across_row[:, BLK - 1 :] - down_col), 0.0
            )
            w = (lk[r, c].astype(F32) * tail).astype(BF16)
            ups.append(mm(w, lv[r, c], ATB))
        first_up[h] = ups[0]
        whole = kept(base + BLK, base + TOK - 1) * through(1, h) * ups[0] + ups[1]
        row_st[0, h * DH : (h + 1) * DH] = whole.astype(BF16)
        if h == 0:
            pass_far(0)
            lax.fori_loop(NEAR + 1, n_hi + 1, lambda d, c: (y_copy(d).start(), c)[1], 0)
            pass_own(1)
    pad_row = lax.broadcasted_iota(jnp.int32, (16, DH), 0)

    def factor_rows(f0, f1):
        hi0, hi1 = f0.astype(BF16).astype(F32), f1.astype(BF16).astype(F32)
        out = jnp.where(pad_row == 0, hi0, 0.0)
        out = jnp.where(pad_row == 1, f0 - hi0, out)
        out = jnp.where(pad_row == 2, hi1, out)
        return jnp.where(pad_row == 3, f1 - hi1, out).astype(BF16)

    row_st[0, 2 * DH :] = factor_rows(through(0, 0) * through(1, 0), through(0, 1) * through(1, 1))
    for k in range(1, 4):
        r_copy(k).start()

    def factor_of(block, h):
        tail = block[2 * DH :].astype(F32)
        return tail[2 * h : 2 * h + 1] + tail[2 * h + 1 : 2 * h + 2]

    def keys_of(d):
        quarters = [kv[d, i, :32] for i in range(4)]
        ids = doc_id((me - d) * TOK + lax.broadcasted_iota(jnp.int32, (16, TOK), 1))
        which = lax.broadcasted_iota(jnp.int32, (16, TOK), 0)
        block = jnp.where((which < 4) & (which != ids), -BIG, 0.0).astype(BF16)
        return jnp.concatenate(quarters + [block, jnp.zeros((DH - 16, TOK), BF16)], axis=0)

    def values_of(d):
        quarters = [kv[d, i, 32:] for i in range(4)]
        return jnp.concatenate(quarters + [jnp.ones((DH, TOK), BF16)], axis=0)

    def arrived(d):
        s_copy(d).wait_recv()
        t_copy(d).wait_recv()

    def diagonal():
        keys, values = keys_of(0), values_of(0)
        for t in range(4):
            r = slice(t * HALF, (t + 1) * HALF)
            s = mm(qx[r], keys)
            pos = (t % 2) * HALF + lax.broadcasted_iota(jnp.int32, (HALF, TOK), 0)
            s = jnp.where(lax.broadcasted_iota(jnp.int32, (HALF, TOK), 1) <= pos, s, -BIG)
            m = jnp.max(s, axis=1, keepdims=True)
            p = jnp.exp2((s - m) * SCALE).astype(BF16)
            acc[r] = mm(p, values, ABT)
            top[r] = jnp.broadcast_to(m, (HALF, DH))

    def visit(d):
        keys, values = keys_of(d), values_of(d)
        for t in range(4):
            r = slice(t * HALF, (t + 1) * HALF)
            s = mm(qx[r], keys)
            old = top[r, :1]
            m = jnp.maximum(old, jnp.max(s, axis=1, keepdims=True))
            p = jnp.exp2((s - m) * SCALE).astype(BF16)
            acc[r] = jnp.exp2((old - m) * SCALE) * acc[r] + mm(p, values, ABT)
            top[r] = jnp.broadcast_to(m, (HALF, DH))

    pass_own(2)
    arrived(0)
    diagonal()
    for d in range(3, LOOK + 1):
        pass_own(d)
    pass_far(1)

    for k in range(1, 4):
        r_copy(k).wait_recv()
    line_first = line * 4 * TOK
    enter_row = []
    enter_factor = []
    for h in range(2):
        total = jnp.zeros((DH, DH), F32)
        before = jnp.zeros((DH, DH), F32)
        factor = jnp.ones((1, DH), F32)
        factor_before = jnp.ones((1, DH), F32)
        plain = jnp.ones((1, DH), F32)
        for x in range(4):
            block = row_st[lax.rem(col - x + 4, 4)]
            own = col == x
            before = jnp.where(own, total, before)
            factor_before = jnp.where(own, factor, factor_before)
            f = factor_of(block, h)
            fk = f * kept(line_first + x * TOK, line_first + (x + 1) * TOK - 1)
            total = fk * total + block[h * DH : (h + 1) * DH].astype(F32)
            factor = factor * fk
            plain = plain * f
        carry[h] = before
        enter_factor.append(factor_before)
        enter_row.append(plain)
        col_st[0, h * DH : (h + 1) * DH] = total.astype(BF16)
    col_st[0, 2 * DH :] = factor_rows(enter_row[0], enter_row[1])
    n_down = 3 - line
    lax.fori_loop(1, n_down + 1, lambda k, c: (c_copy(k).start(), c)[1], 0)

    def loop_body(d, c):
        pass_own(d + LOOK)
        pass_far(d + 1)
        arrived(d)
        visit(d)
        return c

    early = jnp.minimum(n_lo, 2)
    lax.fori_loop(1, early + 1, loop_body, 0)

    def column(i, state):
        k = line - i
        c_copy(k).wait_recv()
        block = col_st[k]
        first = i * 4 * TOK
        keep = kept(first, first + 4 * TOK - 1)
        return tuple(
            keep * factor_of(block, h) * state[h] + block[h * DH : (h + 1) * DH].astype(F32) for h in range(2)
        )

    entered = lax.fori_loop(0, line, column, (jnp.zeros((DH, DH), F32), jnp.zeros((DH, DH), F32)))
    for h in range(2):
        state = enter_factor[h] * entered[h] + carry[h]
        for b in range(2):
            r, c, _, down_col = parts(b, h)
            first = base + b * BLK
            mine = jnp.where(doc_start(first + col_pos) <= first - 1, jnp.exp(down_col), 0.0)
            full = raw[r, c] + mine * mm(lq[r, c], state.astype(BF16))
            scale = lax.rsqrt(jnp.mean(full * full, axis=1, keepdims=True) + 1e-6)
            lin_out[r, c] = (full * scale * gain[:, c]).astype(BF16)
            if b == 0:
                state = kept(base, base + BLK - 1) * through(0, h) * state + first_up[h]

    lax.fori_loop(early + 1, n_lo + 1, loop_body, 0)

    for t in range(4):
        r = slice(t * HALF, (t + 1) * HALF)
        out = acc[r, :DH] / acc[r, DH:]
        h, b = t // 2, t % 2
        soft_out[b * HALF : (b + 1) * HALF, h * DH : (h + 1) * DH] = out.astype(BF16)

    def sent(d, c):
        s_copy(d).wait_send()
        pl.when(d <= NEAR)(lambda: z_copy(d).wait_send())
        t_copy(d).wait_send()
        return c

    lax.fori_loop(0, n_lo + 1, sent, 0)
    lax.fori_loop(1, n_hi + 1, lambda d, c: (x_copy(d).wait_send(), c)[1], 0)
    lax.fori_loop(NEAR + 1, n_hi + 1, lambda d, c: (y_copy(d).wait_send(), c)[1], 0)
    for k in range(1, 4):
        r_copy(k).wait_send()
    lax.fori_loop(1, n_down + 1, lambda k, c: (c_copy(k).wait_send(), c)[1], 0)


def local(doc_lengths, lin_q, lin_k, lin_v, log_decay, lin_gain, soft_q, soft_k, soft_v):
    vmem = pltpu.VMEM
    dma = pltpu.SemaphoreType.DMA
    wide = (TOK, 2 * DH)
    slots = REACH + 1
    return pl.pallas_call(
        kernel,
        out_shape=(jax.ShapeDtypeStruct(wide, BF16), jax.ShapeDtypeStruct(wide, BF16)),
        in_specs=[pl.BlockSpec(memory_space=pltpu.SMEM)] + [pl.BlockSpec(memory_space=pl.ANY)] * 8,
        out_specs=(pl.BlockSpec(memory_space=vmem), pl.BlockSpec(memory_space=vmem)),
        scratch_shapes=[
            vmem(wide, BF16), vmem(wide, BF16), vmem(wide, BF16), vmem((2, TOK), F32), vmem((1, 2 * DH), F32),
            vmem(wide, BF16),
            vmem((slots, 4, 64, TOK), BF16), vmem((2 * TOK, 2 * DH), BF16), vmem((2 * TOK, DH), F32),
            vmem((2 * TOK, 2 * DH), F32), vmem(wide, F32), vmem((BLK, 8), F32),
            vmem((4, 2 * DH + 16, DH), BF16), vmem((4, 2 * DH + 16, DH), BF16), vmem((2, DH, DH), F32),
            vmem((2, DH, DH), F32),
            dma((8,)), dma((slots,)), dma((slots,)), dma((slots,)), dma((slots,)), dma((slots,)), dma((slots,)),
            dma((slots,)), dma((slots,)), dma((slots,)), dma((4,)), dma((4,)), dma((4,)), dma((4,)),
        ],
        compiler_params=pltpu.CompilerParams(
            collective_id=0, has_side_effects=True, vmem_limit_bytes=60 * 1024 * 1024
        ),
    )(doc_lengths, lin_q, lin_k, lin_v, log_decay, lin_gain.reshape(1, 2 * DH), soft_q, soft_k.T, soft_v.T)


def solution(mesh):
    both = P("ctx", "head")
    return jax.shard_map(
        local,
        mesh=mesh,
        in_specs=(P(), both, both, both, P("head", "ctx"), P("head"), both, both, both),
        out_specs=(both, both),
        check_vma=False,
    )
```

```python
import math

import jax
import jax.numpy as jnp
from jax import lax
from jax.experimental import pallas as pl
from jax.experimental.pallas import tpu as pltpu
from jax.sharding import PartitionSpec as P

DH = 128
BLK = 256
TOK = 512
ROW_AT, COLUMN_AT = 4, 9
NEAR = 9
LOOK = 4
REACH = 12
HALF = 256
BIG = 1048576.0
SCALE = math.log2(math.e) / math.sqrt(DH)
MESH = pl.DeviceIdType.MESH
F32 = jnp.float32
BF16 = jnp.bfloat16
AB = (((1,), (0,)), ((), ()))
ABT = (((1,), (1,)), ((), ()))
ATB = (((0,), (0,)), ((), ()))


def mm(a, b, dims=AB):
    return lax.dot_general(a, b, dims, preferred_element_type=F32)


def kernel(
    doc, lq_in, lk_in, lv_in, ld_in, gain_in, sq_in, sk_in, sv_in,
    lin_out, soft_out,
    lq, lk, lv, ld, gain, sq,
    kv, qx, top, acc, raw, cum, row_st, col_st, first_up, carry,
    in_sem, x_send, x_recv, y_send, s_send, s_recv, z_send, z_recv, t_send, t_recv,
    r_send, r_recv, c_send, c_recv,
):
    me = lax.axis_index("ctx")
    hd = lax.axis_index("head")
    col, line = lax.rem(me, 4), me // 4
    sib = hd + 1 - 2 * lax.rem(hd, 2)
    zp = hd + 2 - 4 * lax.rem(hd // 2, 2)
    quarter = lax.rem(hd, 4)
    zquarter = lax.rem(zp, 4)
    n_lo = jnp.minimum(me, REACH)
    n_hi = jnp.minimum(15 - me, REACH)

    loads = [
        pltpu.make_async_copy(a, b, in_sem.at[i])
        for i, (a, b) in enumerate(
            [(sk_in, kv.at[0, quarter, :32]), (sv_in, kv.at[0, quarter, 32:]), (sq_in, sq), (lq_in, lq), (lk_in, lk), (lv_in, lv), (ld_in, ld), (gain_in, gain)]
        )
    ]
    for load in loads:
        load.start()

    barrier = pltpu.get_barrier_semaphore()

    def greet(ctx, head):
        pl.semaphore_signal(barrier, inc=1, device_id=(ctx, head), device_id_type=MESH)

    greet(me, sib)
    greet(me, zp)
    lax.fori_loop(1, n_lo + 1, lambda d, c: (greet(me - d, hd), c)[1], 0)
    lax.fori_loop(1, n_hi + 1, lambda d, c: (greet(me + d, hd), c)[1], 0)

    loads[0].wait()
    loads[1].wait()
    pl.semaphore_wait(barrier, 2 + n_lo + n_hi)

    def copy(src, dst, send, recv, ctx, head):
        return pltpu.make_async_remote_copy(
            src_ref=src, dst_ref=dst, send_sem=send, recv_sem=recv, device_id=(ctx, head), device_id_type=MESH
        )

    def x_copy(d):
        return copy(kv.at[0, quarter], kv.at[d, quarter], x_send.at[d], x_recv.at[d], me + d, hd)

    def y_copy(d):
        return copy(kv.at[0, zquarter], kv.at[d, zquarter], y_send.at[d], z_recv.at[d], me + d, hd)

    def s_copy(d):
        return copy(kv.at[d, quarter], kv.at[d, quarter], s_send.at[d], s_recv.at[d], me, sib)

    def z_copy(d):
        return copy(kv.at[d, quarter], kv.at[d, quarter], z_send.at[d], z_recv.at[d], me, zp)

    def t_copy(d):
        return copy(kv.at[d, zquarter], kv.at[d, zquarter], t_send.at[d], t_recv.at[d], me, sib)

    def r_copy(k):
        return copy(row_st.at[0], row_st.at[k], r_send.at[k], r_recv.at[k], line * 4 + lax.rem(col + k, 4), hd)

    def c_copy(k):
        return copy(col_st.at[0], col_st.at[k], c_send.at[k], c_recv.at[k], me + 4 * k, hd)

    def pass_own(d):
        @pl.when(d <= n_lo)
        def _():
            x_copy(d).wait_recv()
            s_copy(d).start()
            pl.when(d <= NEAR)(lambda: z_copy(d).start())

    def pass_far(d):
        @pl.when(d <= n_lo)
        def _():
            z_copy(d).wait_recv()
            t_copy(d).start()

    s_copy(0).start()
    z_copy(0).start()
    lax.fori_loop(1, n_hi + 1, lambda d, c: (x_copy(d).start(), c)[1], 0)

    bounds = [doc[0], doc[0] + doc[1], doc[0] + doc[1] + doc[2]]

    def doc_start(p):
        start = jnp.zeros_like(p)
        for b in bounds:
            start = jnp.maximum(start, jnp.where(b <= p, b, 0))
        return start

    def doc_id(p):
        count = jnp.zeros_like(p)
        for b in bounds:
            count = count + jnp.where(b <= p, 1, 0)
        return count

    base = me * TOK

    loads[2].wait()
    rows = base + lax.broadcasted_iota(jnp.int32, (TOK, DH), 0)
    lanes = lax.broadcasted_iota(jnp.int32, (TOK, DH), 1)
    marks = jnp.where(doc_id(rows) == lanes, 1.0, 0.0).astype(BF16)
    for h in range(2):
        qx[h * TOK : (h + 1) * TOK, :DH] = sq[:, h * DH : (h + 1) * DH]
        qx[h * TOK : (h + 1) * TOK, DH:] = marks

    for load in loads[3:]:
        load.wait()
    tri = jnp.where(
        lax.broadcasted_iota(jnp.int32, (BLK, BLK), 0) <= lax.broadcasted_iota(jnp.int32, (BLK, BLK), 1), 1.0, 0.0
    ).astype(F32)
    steps = jnp.concatenate([ld[:, :BLK], ld[:, BLK:], jnp.zeros((4, BLK), F32)], axis=0)
    running = lax.dot_general(steps, tri, AB, precision=lax.Precision.HIGHEST, preferred_element_type=F32)
    cum[...] = running.T
    row_of = lax.broadcasted_iota(jnp.int32, (BLK, BLK), 0)
    col_of = lax.broadcasted_iota(jnp.int32, (BLK, BLK), 1)
    col_pos = lax.broadcasted_iota(jnp.int32, (BLK, 1), 0)

    def parts(b, h):
        r = slice(b * BLK, (b + 1) * BLK)
        c = slice(h * DH, (h + 1) * DH)
        return r, c, running[2 * b + h : 2 * b + h + 1, :], cum[:, 2 * b + h : 2 * b + h + 1]

    def through(b, h):
        end = running[2 * b + h : 2 * b + h + 1, BLK - 1 :]
        return jnp.exp(end)

    def kept(first, last):
        return jnp.where(doc_start(last) <= first - 1, 1.0, 0.0).astype(F32)

    for h in range(2):
        ups = []
        for b in range(2):
            r, c, across_row, down_col = parts(b, h)
            first = base + b * BLK
            start = doc_start(first + col_pos) - first
            allowed = (col_of <= row_of) & (col_of >= start)
            decays = jnp.exp(down_col - across_row)
            a = jnp.where(allowed, mm(lq[r, c], lk[r, c], ABT) * decays, 0.0).astype(BF16)
            raw[r, c] = mm(a, lv[r, c])
            tail = jnp.where(
                first + col_pos >= doc_start(first + BLK - 1), jnp.exp(across_row[:, BLK - 1 :] - down_col), 0.0
            )
            w = (lk[r, c].astype(F32) * tail).astype(BF16)
            ups.append(mm(w, lv[r, c], ATB))
        first_up[h] = ups[0]
        whole = kept(base + BLK, base + TOK - 1) * through(1, h) * ups[0] + ups[1]
        row_st[0, h * DH : (h + 1) * DH] = whole.astype(BF16)
        if h == 0:
            pass_far(0)
            lax.fori_loop(NEAR + 1, n_hi + 1, lambda d, c: (y_copy(d).start(), c)[1], 0)
            pass_own(1)
    pad_row = lax.broadcasted_iota(jnp.int32, (16, DH), 0)

    def factor_rows(f0, f1):
        hi0, hi1 = f0.astype(BF16).astype(F32), f1.astype(BF16).astype(F32)
        out = jnp.where(pad_row == 0, hi0, 0.0)
        out = jnp.where(pad_row == 1, f0 - hi0, out)
        out = jnp.where(pad_row == 2, hi1, out)
        return jnp.where(pad_row == 3, f1 - hi1, out).astype(BF16)

    row_st[0, 2 * DH :] = factor_rows(through(0, 0) * through(1, 0), through(0, 1) * through(1, 1))
    for k in range(1, 4):
        r_copy(k).start()

    def factor_of(block, h):
        tail = block[2 * DH :].astype(F32)
        return tail[2 * h : 2 * h + 1] + tail[2 * h + 1 : 2 * h + 2]

    def keys_of(d):
        quarters = [kv[d, i, :32] for i in range(4)]
        ids = doc_id((me - d) * TOK + lax.broadcasted_iota(jnp.int32, (16, TOK), 1))
        which = lax.broadcasted_iota(jnp.int32, (16, TOK), 0)
        block = jnp.where((which < 4) & (which != ids), -BIG, 0.0).astype(BF16)
        return jnp.concatenate(quarters + [block, jnp.zeros((DH - 16, TOK), BF16)], axis=0)

    def values_of(d):
        quarters = [kv[d, i, 32:] for i in range(4)]
        return jnp.concatenate(quarters + [jnp.ones((DH, TOK), BF16)], axis=0)

    def arrived(d):
        s_copy(d).wait_recv()
        t_copy(d).wait_recv()

    def diagonal():
        keys, values = keys_of(0), values_of(0)
        for t in range(4):
            r = slice(t * HALF, (t + 1) * HALF)
            s = mm(qx[r], keys)
            pos = (t % 2) * HALF + lax.broadcasted_iota(jnp.int32, (HALF, TOK), 0)
            s = jnp.where(lax.broadcasted_iota(jnp.int32, (HALF, TOK), 1) <= pos, s, -BIG)
            m = jnp.max(s, axis=1, keepdims=True)
            p = jnp.exp2((s - m) * SCALE).astype(BF16)
            acc[r] = mm(p, values, ABT)
            top[r] = jnp.broadcast_to(m, (HALF, DH))

    def visit(d):
        keys, values = keys_of(d), values_of(d)
        tiles = [slice(t * HALF, (t + 1) * HALF) for t in range(2 * TOK // HALF)]
        scores = mm(qx[tiles[0]], keys)
        for t, r in enumerate(tiles):
            s = scores
            if t + 1 < len(tiles):
                scores = mm(qx[tiles[t + 1]], keys)
            old = top[r]
            m = jnp.maximum(old, jnp.max(s, axis=1, keepdims=True))
            top[r] = m
            p = jnp.exp2((s - jnp.concatenate([m] * (TOK // DH), axis=1)) * SCALE).astype(BF16)
            shrink = jnp.exp2((old - m) * SCALE)
            acc[r] = jnp.concatenate([shrink, shrink], axis=1) * acc[r] + mm(p, values, ABT)

    pass_own(2)
    arrived(0)
    diagonal()
    for d in range(3, LOOK + 1):
        pass_own(d)
    pass_far(1)

    def loop_body(d, c):
        pass_own(d + LOOK)
        pass_far(d + 1)
        arrived(d)
        visit(d)
        return c

    early = jnp.minimum(n_lo, ROW_AT)
    late = jnp.minimum(n_lo, COLUMN_AT)
    lax.fori_loop(1, early + 1, loop_body, 0)

    for k in range(1, 4):
        r_copy(k).wait_recv()
    line_first = line * 4 * TOK
    enter_row = []
    enter_factor = []
    for h in range(2):
        total = jnp.zeros((DH, DH), F32)
        before = jnp.zeros((DH, DH), F32)
        factor = jnp.ones((1, DH), F32)
        factor_before = jnp.ones((1, DH), F32)
        plain = jnp.ones((1, DH), F32)
        for x in range(4):
            block = row_st[lax.rem(col - x + 4, 4)]
            own = col == x
            before = jnp.where(own, total, before)
            factor_before = jnp.where(own, factor, factor_before)
            f = factor_of(block, h)
            fk = f * kept(line_first + x * TOK, line_first + (x + 1) * TOK - 1)
            total = fk * total + block[h * DH : (h + 1) * DH].astype(F32)
            factor = factor * fk
            plain = plain * f
        carry[h] = before
        enter_factor.append(factor_before)
        enter_row.append(plain)
        col_st[0, h * DH : (h + 1) * DH] = total.astype(BF16)
    col_st[0, 2 * DH :] = factor_rows(enter_row[0], enter_row[1])
    n_down = 3 - line
    lax.fori_loop(1, n_down + 1, lambda k, c: (c_copy(k).start(), c)[1], 0)

    lax.fori_loop(early + 1, late + 1, loop_body, 0)

    def column(i, state):
        k = line - i
        c_copy(k).wait_recv()
        block = col_st[k]
        first = i * 4 * TOK
        keep = kept(first, first + 4 * TOK - 1)
        return tuple(
            keep * factor_of(block, h) * state[h] + block[h * DH : (h + 1) * DH].astype(F32) for h in range(2)
        )

    entered = lax.fori_loop(0, line, column, (jnp.zeros((DH, DH), F32), jnp.zeros((DH, DH), F32)))
    for h in range(2):
        state = enter_factor[h] * entered[h] + carry[h]
        for b in range(2):
            r, c, _, down_col = parts(b, h)
            first = base + b * BLK
            mine = jnp.where(doc_start(first + col_pos) <= first - 1, jnp.exp(down_col), 0.0)
            full = raw[r, c] + mine * mm(lq[r, c], state.astype(BF16))
            scale = lax.rsqrt(jnp.mean(full * full, axis=1, keepdims=True) + 1e-6)
            lin_out[r, c] = (full * scale * gain[:, c]).astype(BF16)
            if b == 0:
                state = kept(base, base + BLK - 1) * through(0, h) * state + first_up[h]

    lax.fori_loop(late + 1, n_lo + 1, loop_body, 0)

    for t in range(4):
        r = slice(t * HALF, (t + 1) * HALF)
        out = acc[r, :DH] / acc[r, DH:]
        h, b = t // 2, t % 2
        soft_out[b * HALF : (b + 1) * HALF, h * DH : (h + 1) * DH] = out.astype(BF16)

    def sent(d, c):
        s_copy(d).wait_send()
        pl.when(d <= NEAR)(lambda: z_copy(d).wait_send())
        t_copy(d).wait_send()
        return c

    lax.fori_loop(0, n_lo + 1, sent, 0)
    lax.fori_loop(1, n_hi + 1, lambda d, c: (x_copy(d).wait_send(), c)[1], 0)
    lax.fori_loop(NEAR + 1, n_hi + 1, lambda d, c: (y_copy(d).wait_send(), c)[1], 0)
    for k in range(1, 4):
        r_copy(k).wait_send()
    lax.fori_loop(1, n_down + 1, lambda k, c: (c_copy(k).wait_send(), c)[1], 0)


def local(doc_lengths, lin_q, lin_k, lin_v, log_decay, lin_gain, soft_q, soft_k, soft_v):
    vmem = pltpu.VMEM
    dma = pltpu.SemaphoreType.DMA
    wide = (TOK, 2 * DH)
    slots = REACH + 1
    return pl.pallas_call(
        kernel,
        out_shape=(jax.ShapeDtypeStruct(wide, BF16), jax.ShapeDtypeStruct(wide, BF16)),
        in_specs=[pl.BlockSpec(memory_space=pltpu.SMEM)] + [pl.BlockSpec(memory_space=pl.ANY)] * 8,
        out_specs=(pl.BlockSpec(memory_space=vmem), pl.BlockSpec(memory_space=vmem)),
        scratch_shapes=[
            vmem(wide, BF16), vmem(wide, BF16), vmem(wide, BF16), vmem((2, TOK), F32), vmem((1, 2 * DH), F32),
            vmem(wide, BF16),
            vmem((slots, 4, 64, TOK), BF16), vmem((2 * TOK, 2 * DH), BF16), vmem((2 * TOK, DH), F32),
            vmem((2 * TOK, 2 * DH), F32), vmem(wide, F32), vmem((BLK, 8), F32),
            vmem((4, 2 * DH + 16, DH), BF16), vmem((4, 2 * DH + 16, DH), BF16), vmem((2, DH, DH), F32),
            vmem((2, DH, DH), F32),
            dma((8,)), dma((slots,)), dma((slots,)), dma((slots,)), dma((slots,)), dma((slots,)), dma((slots,)),
            dma((slots,)), dma((slots,)), dma((slots,)), dma((4,)), dma((4,)), dma((4,)), dma((4,)),
        ],
        compiler_params=pltpu.CompilerParams(
            collective_id=0, has_side_effects=True, vmem_limit_bytes=60 * 1024 * 1024
        ),
    )(doc_lengths, lin_q, lin_k, lin_v, log_decay, lin_gain.reshape(1, 2 * DH), soft_q, soft_k.T, soft_v.T)


def solution(mesh):
    both = P("ctx", "head")
    return jax.shard_map(
        local,
        mesh=mesh,
        in_specs=(P(), both, both, both, P("head", "ctx"), P("head"), both, both, both),
        out_specs=(both, both),
        check_vma=False,
    )
```

```python
import math

import jax
import jax.numpy as jnp
from jax import lax
from jax.experimental import pallas as pl
from jax.experimental.pallas import tpu as pltpu
from jax.sharding import PartitionSpec as P

DH = 128
BLK = 256
TOK = 512
ROW_AT, COLUMN_AT = 4, 9
PAIRED = 3
LOOK = 4
REACH = 12
HALF = 256
BIG = 1048576.0
SCALE = math.log2(math.e) / math.sqrt(DH)
MESH = pl.DeviceIdType.MESH
F32 = jnp.float32
BF16 = jnp.bfloat16
AB = (((1,), (0,)), ((), ()))
ABT = (((1,), (1,)), ((), ()))
ATB = (((0,), (0,)), ((), ()))


def mm(a, b, dims=AB):
    return lax.dot_general(a, b, dims, preferred_element_type=F32)


def kernel(
    doc, lq_in, lk_in, lv_in, ld_in, gain_in, sq_in, sk_in, sv_in,
    lin_out, soft_out,
    lq, lk, lv, ld, gain, sq,
    kv, qx, top, acc, raw, cum, row_st, col_st, first_up, carry,
    in_sem, x_send, x_recv, y_send, a_send, s_send, s_recv, z_send, z_recv, t_send, t_recv,
    r_send, r_recv, c_send, c_recv,
):
    me = lax.axis_index("ctx")
    hd = lax.axis_index("head")
    col, line = lax.rem(me, 4), me // 4
    sib = hd + 1 - 2 * lax.rem(hd, 2)
    zp = hd + 2 - 4 * lax.rem(hd // 2, 2)
    quarter = lax.rem(hd, 4)
    zquarter = lax.rem(zp, 4)
    n_lo = jnp.minimum(me, REACH)
    n_hi = jnp.minimum(15 - me, REACH)

    loads = [
        pltpu.make_async_copy(a, b, in_sem.at[i])
        for i, (a, b) in enumerate(
            [(sk_in, kv.at[0, quarter, :32]), (sv_in, kv.at[0, quarter, 32:]), (sq_in, sq), (lq_in, lq), (lk_in, lk), (lv_in, lv), (ld_in, ld), (gain_in, gain)]
        )
    ]
    for load in loads:
        load.start()

    barrier = pltpu.get_barrier_semaphore()

    def greet(ctx, head):
        pl.semaphore_signal(barrier, inc=1, device_id=(ctx, head), device_id_type=MESH)

    greet(me, sib)
    greet(me, zp)
    lax.fori_loop(1, n_lo + 1, lambda d, c: (greet(me - d, hd), c)[1], 0)
    right = jnp.where(line < 3, 3 - col, 0)
    lax.fori_loop(1, right + 1, lambda k, c: (greet(me + k, hd), c)[1], 0)

    loads[0].wait()
    loads[1].wait()
    pl.semaphore_wait(barrier, 2 + n_hi + jnp.where(line < 3, col, 0))

    def copy(src, dst, send, recv, ctx, head):
        return pltpu.make_async_remote_copy(
            src_ref=src, dst_ref=dst, send_sem=send, recv_sem=recv, device_id=(ctx, head), device_id_type=MESH
        )

    def x_copy(d):
        return copy(kv.at[0, quarter], kv.at[d, quarter], x_send.at[0], x_recv.at[d], me, sib)

    def down(k):
        return copy(kv.at[0, quarter], kv.at[4 * k, quarter], x_send.at[k], x_recv.at[4 * k], me + 4 * k, hd)

    def down_far():
        d = 4 * PAIRED
        return copy(kv.at[0, zquarter], kv.at[d, zquarter], y_send.at[0], z_recv.at[d], me + d, hd)

    def aside(k, shift):
        d = 4 * k + shift
        return copy(kv.at[4 * k, quarter], kv.at[d, quarter], a_send.at[k, shift + 3], x_recv.at[d], me + shift, hd)

    def near(shift):
        d = 4 + shift
        return copy(kv.at[0, quarter], kv.at[d, quarter], a_send.at[1, shift + 3], x_recv.at[d], me + d, hd)

    def all_near(use):
        for shift in range(-3, 4):

            @pl.when((line < 3) & (col + shift >= 0) & (col + shift <= 3))
            def _():
                use(shift)

    def aside_far(shift):
        k, d = PAIRED, 4 * PAIRED + shift
        return copy(kv.at[4 * k, zquarter], kv.at[d, zquarter], y_send.at[shift + 4], z_recv.at[d], me + shift, hd)

    def far(d):
        return line - (me - d) // 4 == PAIRED

    def all_aside(k, use):
        for shift in range(-3, 4):
            if shift and 1 <= 4 * k + shift <= REACH:

                @pl.when((line >= k) & (col + shift >= 0) & (col + shift <= 3))
                def _():
                    use(shift)

    def s_copy(d):
        return copy(kv.at[d, quarter], kv.at[d, quarter], s_send.at[d], s_recv.at[d], me, sib)

    def z_copy(d):
        return copy(kv.at[d, quarter], kv.at[d, quarter], z_send.at[d], z_recv.at[d], me, zp)

    def t_copy(d):
        return copy(kv.at[d, zquarter], kv.at[d, zquarter], t_send.at[d], t_recv.at[d], me, sib)

    def r_copy(k):
        return copy(row_st.at[0], row_st.at[k], r_send.at[k], r_recv.at[k], line * 4 + lax.rem(col + k, 4), hd)

    def c_copy(k):
        return copy(col_st.at[0], col_st.at[k], c_send.at[k], c_recv.at[k], me + 4 * k, hd)

    def pass_own(d):
        @pl.when(d <= n_lo)
        def _():
            pl.when((d != 8) & (d != 12))(lambda: x_copy(d).wait_recv())
            s_copy(d).start()
            pl.when(~far(d))(lambda: z_copy(d).start())

    def pass_far(d):
        @pl.when(d <= n_lo)
        def _():
            z_copy(d).wait_recv()
            t_copy(d).start()

    s_copy(0).start()
    z_copy(0).start()
    n_down = 3 - line
    all_aside(0, lambda shift: aside(0, shift).start())
    lax.fori_loop(2, n_down + 1, lambda k, c: (down(k).start(), c)[1], 0)
    all_near(lambda shift: near(shift).start())

    def spread(k):
        pl.when(line >= k)(lambda: x_copy(4 * k).wait_recv())
        all_aside(k, lambda shift: aside(k, shift).start())

    bounds = [doc[0], doc[0] + doc[1], doc[0] + doc[1] + doc[2]]

    def doc_start(p):
        start = jnp.zeros_like(p)
        for b in bounds:
            start = jnp.maximum(start, jnp.where(b <= p, b, 0))
        return start

    def doc_id(p):
        count = jnp.zeros_like(p)
        for b in bounds:
            count = count + jnp.where(b <= p, 1, 0)
        return count

    base = me * TOK

    loads[2].wait()
    rows = base + lax.broadcasted_iota(jnp.int32, (TOK, DH), 0)
    lanes = lax.broadcasted_iota(jnp.int32, (TOK, DH), 1)
    marks = jnp.where(doc_id(rows) == lanes, 1.0, 0.0).astype(BF16)
    for h in range(2):
        qx[h * TOK : (h + 1) * TOK, :DH] = sq[:, h * DH : (h + 1) * DH]
        qx[h * TOK : (h + 1) * TOK, DH:] = marks

    for load in loads[3:]:
        load.wait()
    tri = jnp.where(
        lax.broadcasted_iota(jnp.int32, (BLK, BLK), 0) <= lax.broadcasted_iota(jnp.int32, (BLK, BLK), 1), 1.0, 0.0
    ).astype(F32)
    steps = jnp.concatenate([ld[:, :BLK], ld[:, BLK:], jnp.zeros((4, BLK), F32)], axis=0)
    running = lax.dot_general(steps, tri, AB, precision=lax.Precision.HIGHEST, preferred_element_type=F32)
    cum[...] = running.T
    row_of = lax.broadcasted_iota(jnp.int32, (BLK, BLK), 0)
    col_of = lax.broadcasted_iota(jnp.int32, (BLK, BLK), 1)
    col_pos = lax.broadcasted_iota(jnp.int32, (BLK, 1), 0)

    def parts(b, h):
        r = slice(b * BLK, (b + 1) * BLK)
        c = slice(h * DH, (h + 1) * DH)
        return r, c, running[2 * b + h : 2 * b + h + 1, :], cum[:, 2 * b + h : 2 * b + h + 1]

    def through(b, h):
        end = running[2 * b + h : 2 * b + h + 1, BLK - 1 :]
        return jnp.exp(end)

    def kept(first, last):
        return jnp.where(doc_start(last) <= first - 1, 1.0, 0.0).astype(F32)

    for h in range(2):
        ups = []
        for b in range(2):
            r, c, across_row, down_col = parts(b, h)
            first = base + b * BLK
            start = doc_start(first + col_pos) - first
            allowed = (col_of <= row_of) & (col_of >= start)
            decays = jnp.exp(down_col - across_row)
            a = jnp.where(allowed, mm(lq[r, c], lk[r, c], ABT) * decays, 0.0).astype(BF16)
            raw[r, c] = mm(a, lv[r, c])
            tail = jnp.where(
                first + col_pos >= doc_start(first + BLK - 1), jnp.exp(across_row[:, BLK - 1 :] - down_col), 0.0
            )
            w = (lk[r, c].astype(F32) * tail).astype(BF16)
            ups.append(mm(w, lv[r, c], ATB))
        first_up[h] = ups[0]
        whole = kept(base + BLK, base + TOK - 1) * through(1, h) * ups[0] + ups[1]
        row_st[0, h * DH : (h + 1) * DH] = whole.astype(BF16)
        if h == 0:
            pass_far(0)
            pl.when(line + PAIRED <= 3)(lambda: down_far().start())
            for k in range(2, 4):
                spread(k)
            pass_own(1)
    pad_row = lax.broadcasted_iota(jnp.int32, (16, DH), 0)

    def factor_rows(f0, f1):
        hi0, hi1 = f0.astype(BF16).astype(F32), f1.astype(BF16).astype(F32)
        out = jnp.where(pad_row == 0, hi0, 0.0)
        out = jnp.where(pad_row == 1, f0 - hi0, out)
        out = jnp.where(pad_row == 2, hi1, out)
        return jnp.where(pad_row == 3, f1 - hi1, out).astype(BF16)

    row_st[0, 2 * DH :] = factor_rows(through(0, 0) * through(1, 0), through(0, 1) * through(1, 1))
    for k in range(1, 4):
        pl.when((line < 3) | (col + k <= 3))(lambda: r_copy(k).start())

    def factor_of(block, h):
        tail = block[2 * DH :].astype(F32)
        return tail[2 * h : 2 * h + 1] + tail[2 * h + 1 : 2 * h + 2]

    def keys_of(d):
        quarters = [kv[d, i, :32] for i in range(4)]
        ids = doc_id((me - d) * TOK + lax.broadcasted_iota(jnp.int32, (16, TOK), 1))
        which = lax.broadcasted_iota(jnp.int32, (16, TOK), 0)
        block = jnp.where((which < 4) & (which != ids), -BIG, 0.0).astype(BF16)
        return jnp.concatenate(quarters + [block, jnp.zeros((DH - 16, TOK), BF16)], axis=0)

    def values_of(d):
        quarters = [kv[d, i, 32:] for i in range(4)]
        return jnp.concatenate(quarters + [jnp.ones((DH, TOK), BF16)], axis=0)

    def arrived(d):
        s_copy(d).wait_recv()
        t_copy(d).wait_recv()

    def diagonal():
        keys, values = keys_of(0), values_of(0)
        for t in range(4):
            r = slice(t * HALF, (t + 1) * HALF)
            s = mm(qx[r], keys)
            pos = (t % 2) * HALF + lax.broadcasted_iota(jnp.int32, (HALF, TOK), 0)
            s = jnp.where(lax.broadcasted_iota(jnp.int32, (HALF, TOK), 1) <= pos, s, -BIG)
            m = jnp.max(s, axis=1, keepdims=True)
            p = jnp.exp2((s - m) * SCALE).astype(BF16)
            acc[r] = mm(p, values, ABT)
            top[r] = jnp.broadcast_to(m, (HALF, DH))

    def visit(d):
        keys, values = keys_of(d), values_of(d)
        tiles = [slice(t * HALF, (t + 1) * HALF) for t in range(2 * TOK // HALF)]
        scores = mm(qx[tiles[0]], keys)
        for t, r in enumerate(tiles):
            s = scores
            if t + 1 < len(tiles):
                scores = mm(qx[tiles[t + 1]], keys)
            old = top[r]
            m = jnp.maximum(old, jnp.max(s, axis=1, keepdims=True))
            top[r] = m
            p = jnp.exp2((s - jnp.concatenate([m] * (TOK // DH), axis=1)) * SCALE).astype(BF16)
            shrink = jnp.exp2((old - m) * SCALE)
            acc[r] = jnp.concatenate([shrink, shrink], axis=1) * acc[r] + mm(p, values, ABT)

    pass_far(4 * PAIRED)
    all_aside(PAIRED, lambda shift: aside_far(shift).start())
    pass_own(2)
    arrived(0)
    diagonal()
    for d in range(3, LOOK + 1):
        pass_own(d)
    pass_far(1)

    def loop_body(d, c):
        pass_own(d + LOOK)
        pl.when(d + 1 != 4 * PAIRED)(lambda: pass_far(d + 1))
        arrived(d)
        visit(d)
        return c

    early = jnp.minimum(n_lo, ROW_AT)
    late = jnp.minimum(n_lo, COLUMN_AT)
    lax.fori_loop(1, early + 1, loop_body, 0)

    for k in range(1, 4):
        pl.when((line < 3) | (col >= k))(lambda: r_copy(k).wait_recv())
    line_first = line * 4 * TOK
    enter_row = []
    enter_factor = []
    for h in range(2):
        total = jnp.zeros((DH, DH), F32)
        before = jnp.zeros((DH, DH), F32)
        factor = jnp.ones((1, DH), F32)
        factor_before = jnp.ones((1, DH), F32)
        plain = jnp.ones((1, DH), F32)
        for x in range(4):
            block = row_st[lax.rem(col - x + 4, 4)]
            own = col == x
            before = jnp.where(own, total, before)
            factor_before = jnp.where(own, factor, factor_before)
            f = factor_of(block, h)
            fk = f * kept(line_first + x * TOK, line_first + (x + 1) * TOK - 1)
            total = fk * total + block[h * DH : (h + 1) * DH].astype(F32)
            factor = factor * fk
            plain = plain * f
        carry[h] = before
        enter_factor.append(factor_before)
        enter_row.append(plain)
        col_st[0, h * DH : (h + 1) * DH] = total.astype(BF16)
    col_st[0, 2 * DH :] = factor_rows(enter_row[0], enter_row[1])
    lax.fori_loop(1, n_down + 1, lambda k, c: (c_copy(k).start(), c)[1], 0)

    lax.fori_loop(early + 1, late + 1, loop_body, 0)

    def column(i, state):
        k = line - i
        c_copy(k).wait_recv()
        block = col_st[k]
        first = i * 4 * TOK
        keep = kept(first, first + 4 * TOK - 1)
        return tuple(
            keep * factor_of(block, h) * state[h] + block[h * DH : (h + 1) * DH].astype(F32) for h in range(2)
        )

    entered = lax.fori_loop(0, line, column, (jnp.zeros((DH, DH), F32), jnp.zeros((DH, DH), F32)))
    for h in range(2):
        state = enter_factor[h] * entered[h] + carry[h]
        for b in range(2):
            r, c, _, down_col = parts(b, h)
            first = base + b * BLK
            mine = jnp.where(doc_start(first + col_pos) <= first - 1, jnp.exp(down_col), 0.0)
            full = raw[r, c] + mine * mm(lq[r, c], state.astype(BF16))
            scale = lax.rsqrt(jnp.mean(full * full, axis=1, keepdims=True) + 1e-6)
            lin_out[r, c] = (full * scale * gain[:, c]).astype(BF16)
            if b == 0:
                state = kept(base, base + BLK - 1) * through(0, h) * state + first_up[h]

    lax.fori_loop(late + 1, n_lo + 1, loop_body, 0)

    for t in range(4):
        r = slice(t * HALF, (t + 1) * HALF)
        out = acc[r, :DH] / acc[r, DH:]
        h, b = t // 2, t % 2
        soft_out[b * HALF : (b + 1) * HALF, h * DH : (h + 1) * DH] = out.astype(BF16)

    def sent(d, c):
        s_copy(d).wait_send()
        pl.when(~far(d))(lambda: z_copy(d).wait_send())
        t_copy(d).wait_send()
        return c

    lax.fori_loop(0, n_lo + 1, sent, 0)
    lax.fori_loop(2, n_down + 1, lambda k, c: (down(k).wait_send(), c)[1], 0)
    all_near(lambda shift: near(shift).wait_send())
    pl.when(line + PAIRED <= 3)(lambda: down_far().wait_send())
    for k in (0, 2, 3):
        all_aside(k, lambda shift: aside(k, shift).wait_send())
    all_aside(PAIRED, lambda shift: aside_far(shift).wait_send())
    for k in range(1, 4):
        pl.when((line < 3) | (col + k <= 3))(lambda: r_copy(k).wait_send())
    lax.fori_loop(1, n_down + 1, lambda k, c: (c_copy(k).wait_send(), c)[1], 0)


def local(doc_lengths, lin_q, lin_k, lin_v, log_decay, lin_gain, soft_q, soft_k, soft_v):
    vmem = pltpu.VMEM
    dma = pltpu.SemaphoreType.DMA
    wide = (TOK, 2 * DH)
    slots = REACH + 1
    return pl.pallas_call(
        kernel,
        out_shape=(jax.ShapeDtypeStruct(wide, BF16), jax.ShapeDtypeStruct(wide, BF16)),
        in_specs=[pl.BlockSpec(memory_space=pltpu.SMEM)] + [pl.BlockSpec(memory_space=pl.ANY)] * 8,
        out_specs=(pl.BlockSpec(memory_space=vmem), pl.BlockSpec(memory_space=vmem)),
        scratch_shapes=[
            vmem(wide, BF16), vmem(wide, BF16), vmem(wide, BF16), vmem((2, TOK), F32), vmem((1, 2 * DH), F32),
            vmem(wide, BF16),
            vmem((slots, 4, 64, TOK), BF16), vmem((2 * TOK, 2 * DH), BF16), vmem((2 * TOK, DH), F32),
            vmem((2 * TOK, 2 * DH), F32), vmem(wide, F32), vmem((BLK, 8), F32),
            vmem((4, 2 * DH + 16, DH), BF16), vmem((4, 2 * DH + 16, DH), BF16), vmem((2, DH, DH), F32),
            vmem((2, DH, DH), F32),
            dma((8,)), dma((4,)), dma((slots,)), dma((8,)), dma((4, 7)), dma((slots,)), dma((slots,)), dma((slots,)),
            dma((slots,)), dma((slots,)), dma((slots,)), dma((4,)), dma((4,)), dma((4,)), dma((4,)),
        ],
        compiler_params=pltpu.CompilerParams(
            collective_id=0, has_side_effects=True, vmem_limit_bytes=60 * 1024 * 1024
        ),
    )(doc_lengths, lin_q, lin_k, lin_v, log_decay, lin_gain.reshape(1, 2 * DH), soft_q, soft_k.T, soft_v.T)


def solution(mesh):
    both = P("ctx", "head")
    return jax.shard_map(
        local,
        mesh=mesh,
        in_specs=(P(), both, both, both, P("head", "ctx"), P("head"), both, both, both),
        out_specs=(both, both),
        check_vma=False,
    )
```

```python
import math

import jax
import jax.numpy as jnp
from jax import lax
from jax.experimental import pallas as pl
from jax.experimental.pallas import tpu as pltpu
from jax.sharding import PartitionSpec as P

DH = 128
BLK = 256
TOK = 512
ROW_AT, COLUMN_AT = 4, 9
PAIRED = 3
LOOK = 3
REACH = 12
HALF = 256
BIG = 1048576.0
SCALE = math.log2(math.e) / math.sqrt(DH)
MESH = pl.DeviceIdType.MESH
F32 = jnp.float32
BF16 = jnp.bfloat16
AB = (((1,), (0,)), ((), ()))
ABT = (((1,), (1,)), ((), ()))
ATB = (((0,), (0,)), ((), ()))


def mm(a, b, dims=AB):
    return lax.dot_general(a, b, dims, preferred_element_type=F32)


def kernel(
    doc, lq_in, lk_in, lv_in, ld_in, gain_in, sq_in, sk_in, sv_in,
    lin_out, soft_out,
    lq, lk, lv, ld, gain, sq,
    kv, qx, top, acc, raw, cum, row_st, col_st, first_up, carry,
    in_sem, x_send, x_recv, y_send, a_send, s_send, s_recv, z_send, z_recv, t_send, t_recv,
    r_send, r_recv, c_send, c_recv,
):
    me = lax.axis_index("ctx")
    hd = lax.axis_index("head")
    col, line = lax.rem(me, 4), me // 4
    sib = hd + 1 - 2 * lax.rem(hd, 2)
    zp = hd + 2 - 4 * lax.rem(hd // 2, 2)
    quarter = lax.rem(hd, 4)
    zquarter = lax.rem(zp, 4)
    n_lo = jnp.minimum(me, REACH)
    n_hi = jnp.minimum(15 - me, REACH)

    loads = [
        pltpu.make_async_copy(a, b, in_sem.at[i])
        for i, (a, b) in enumerate(
            [(sk_in, kv.at[0, quarter, :32]), (sv_in, kv.at[0, quarter, 32:]), (sq_in, sq), (lq_in, lq), (lk_in, lk), (lv_in, lv), (ld_in, ld), (gain_in, gain)]
        )
    ]
    for load in loads:
        load.start()

    barrier = pltpu.get_barrier_semaphore()

    def greet(ctx, head):
        pl.semaphore_signal(barrier, inc=1, device_id=(ctx, head), device_id_type=MESH)

    greet(me, sib)
    greet(me, zp)
    lax.fori_loop(1, n_lo + 1, lambda d, c: (greet(me - d, hd), c)[1], 0)
    right = jnp.where(line < 3, 3 - col, 0)
    lax.fori_loop(1, right + 1, lambda k, c: (greet(me + k, hd), c)[1], 0)

    loads[0].wait()
    loads[1].wait()
    pl.semaphore_wait(barrier, 2 + n_hi + jnp.where(line < 3, col, 0))

    def copy(src, dst, send, recv, ctx, head):
        return pltpu.make_async_remote_copy(
            src_ref=src, dst_ref=dst, send_sem=send, recv_sem=recv, device_id=(ctx, head), device_id_type=MESH
        )

    def x_copy(d):
        return copy(kv.at[0, quarter], kv.at[d, quarter], x_send.at[0], x_recv.at[d], me, sib)

    def down(k):
        return copy(kv.at[0, quarter], kv.at[4 * k, quarter], x_send.at[k], x_recv.at[4 * k], me + 4 * k, hd)

    def down_far():
        d = 4 * PAIRED
        return copy(kv.at[0, zquarter], kv.at[d, zquarter], y_send.at[0], z_recv.at[d], me + d, hd)

    def aside(k, shift):
        d = 4 * k + shift
        return copy(kv.at[4 * k, quarter], kv.at[d, quarter], a_send.at[k, shift + 3], x_recv.at[d], me + shift, hd)

    def near(shift):
        d = 4 + shift
        return copy(kv.at[0, quarter], kv.at[d, quarter], a_send.at[1, shift + 3], x_recv.at[d], me + d, hd)

    def all_near(use):
        for shift in range(-3, 4):

            @pl.when((line < 3) & (col + shift >= 0) & (col + shift <= 3))
            def _():
                use(shift)

    def aside_far(shift):
        k, d = PAIRED, 4 * PAIRED + shift
        return copy(kv.at[4 * k, zquarter], kv.at[d, zquarter], y_send.at[shift + 4], z_recv.at[d], me + shift, hd)

    def far(d):
        return line - (me - d) // 4 == PAIRED

    def all_aside(k, use):
        for shift in range(-3, 4):
            if shift and 1 <= 4 * k + shift <= REACH:

                @pl.when((line >= k) & (col + shift >= 0) & (col + shift <= 3))
                def _():
                    use(shift)

    def s_copy(d):
        return copy(kv.at[d, quarter], kv.at[d, quarter], s_send.at[d], s_recv.at[d], me, sib)

    def z_copy(d):
        return copy(kv.at[d, quarter], kv.at[d, quarter], z_send.at[d], z_recv.at[d], me, zp)

    def t_copy(d):
        return copy(kv.at[d, zquarter], kv.at[d, zquarter], t_send.at[d], t_recv.at[d], me, sib)

    def r_copy(k):
        return copy(row_st.at[0], row_st.at[k], r_send.at[k], r_recv.at[k], line * 4 + lax.rem(col + k, 4), hd)

    def c_copy(k):
        return copy(col_st.at[0], col_st.at[k], c_send.at[k], c_recv.at[k], me + 4 * k, hd)

    def pass_own(d):
        @pl.when(d <= n_lo)
        def _():
            pl.when((d != 8) & (d != 12))(lambda: x_copy(d).wait_recv())
            s_copy(d).start()
            pl.when(~far(d))(lambda: z_copy(d).start())

    def pass_far(d):
        @pl.when(d <= n_lo)
        def _():
            z_copy(d).wait_recv()
            t_copy(d).start()

    s_copy(0).start()
    z_copy(0).start()
    n_down = 3 - line
    all_aside(0, lambda shift: aside(0, shift).start())
    lax.fori_loop(2, n_down + 1, lambda k, c: (down(k).start(), c)[1], 0)
    all_near(lambda shift: near(shift).start())

    def spread(k):
        pl.when(line >= k)(lambda: x_copy(4 * k).wait_recv())
        all_aside(k, lambda shift: aside(k, shift).start())

    bounds = [doc[0], doc[0] + doc[1], doc[0] + doc[1] + doc[2]]

    def doc_start(p):
        start = jnp.zeros_like(p)
        for b in bounds:
            start = jnp.maximum(start, jnp.where(b <= p, b, 0))
        return start

    def doc_id(p):
        count = jnp.zeros_like(p)
        for b in bounds:
            count = count + jnp.where(b <= p, 1, 0)
        return count

    base = me * TOK

    loads[2].wait()
    rows = base + lax.broadcasted_iota(jnp.int32, (TOK, DH), 0)
    lanes = lax.broadcasted_iota(jnp.int32, (TOK, DH), 1)
    marks = jnp.where(doc_id(rows) == lanes, 1.0, 0.0).astype(BF16)
    for h in range(2):
        qx[h * TOK : (h + 1) * TOK, :DH] = sq[:, h * DH : (h + 1) * DH]
        qx[h * TOK : (h + 1) * TOK, DH:] = marks

    for load in loads[3:]:
        load.wait()
    tri = jnp.where(
        lax.broadcasted_iota(jnp.int32, (BLK, BLK), 0) <= lax.broadcasted_iota(jnp.int32, (BLK, BLK), 1), 1.0, 0.0
    ).astype(F32)
    steps = jnp.concatenate([ld[:, :BLK], ld[:, BLK:], jnp.zeros((4, BLK), F32)], axis=0)
    running = lax.dot_general(steps, tri, AB, precision=lax.Precision.HIGHEST, preferred_element_type=F32)
    cum[...] = running.T
    row_of = lax.broadcasted_iota(jnp.int32, (BLK, BLK), 0)
    col_of = lax.broadcasted_iota(jnp.int32, (BLK, BLK), 1)
    col_pos = lax.broadcasted_iota(jnp.int32, (BLK, 1), 0)

    def parts(b, h):
        r = slice(b * BLK, (b + 1) * BLK)
        c = slice(h * DH, (h + 1) * DH)
        return r, c, running[2 * b + h : 2 * b + h + 1, :], cum[:, 2 * b + h : 2 * b + h + 1]

    def through(b, h):
        end = running[2 * b + h : 2 * b + h + 1, BLK - 1 :]
        return jnp.exp(end)

    def kept(first, last):
        return jnp.where(doc_start(last) <= first - 1, 1.0, 0.0).astype(F32)

    for h in range(2):
        ups = []
        for b in range(2):
            r, c, across_row, down_col = parts(b, h)
            first = base + b * BLK
            start = doc_start(first + col_pos) - first
            allowed = (col_of <= row_of) & (col_of >= start)
            decays = jnp.exp(down_col - across_row)
            a = jnp.where(allowed, mm(lq[r, c], lk[r, c], ABT) * decays, 0.0).astype(BF16)
            raw[r, c] = mm(a, lv[r, c])
            tail = jnp.where(
                first + col_pos >= doc_start(first + BLK - 1), jnp.exp(across_row[:, BLK - 1 :] - down_col), 0.0
            )
            w = (lk[r, c].astype(F32) * tail).astype(BF16)
            ups.append(mm(w, lv[r, c], ATB))
        first_up[h] = ups[0]
        whole = kept(base + BLK, base + TOK - 1) * through(1, h) * ups[0] + ups[1]
        row_st[0, h * DH : (h + 1) * DH] = whole.astype(BF16)
        if h == 0:
            pass_far(0)
            pl.when(line + PAIRED <= 3)(lambda: down_far().start())
            for k in range(2, 4):
                spread(k)
            pass_own(1)
    pad_row = lax.broadcasted_iota(jnp.int32, (16, DH), 0)

    def factor_rows(f0, f1):
        hi0, hi1 = f0.astype(BF16).astype(F32), f1.astype(BF16).astype(F32)
        out = jnp.where(pad_row == 0, hi0, 0.0)
        out = jnp.where(pad_row == 1, f0 - hi0, out)
        out = jnp.where(pad_row == 2, hi1, out)
        return jnp.where(pad_row == 3, f1 - hi1, out).astype(BF16)

    row_st[0, 2 * DH :] = factor_rows(through(0, 0) * through(1, 0), through(0, 1) * through(1, 1))
    for k in range(1, 4):
        pl.when((line < 3) | (col + k <= 3))(lambda: r_copy(k).start())

    def factor_of(block, h):
        tail = block[2 * DH :].astype(F32)
        return tail[2 * h : 2 * h + 1] + tail[2 * h + 1 : 2 * h + 2]

    def keys_of(d):
        quarters = [kv[d, i, :32] for i in range(4)]
        ids = doc_id((me - d) * TOK + lax.broadcasted_iota(jnp.int32, (16, TOK), 1))
        which = lax.broadcasted_iota(jnp.int32, (16, TOK), 0)
        block = jnp.where((which < 4) & (which != ids), -BIG, 0.0).astype(BF16)
        return jnp.concatenate(quarters + [block, jnp.zeros((DH - 16, TOK), BF16)], axis=0)

    def values_of(d):
        quarters = [kv[d, i, 32:] for i in range(4)]
        return jnp.concatenate(quarters + [jnp.ones((DH, TOK), BF16)], axis=0)

    def arrived(d):
        s_copy(d).wait_recv()
        t_copy(d).wait_recv()

    def diagonal():
        keys, values = keys_of(0), values_of(0)
        for t in range(4):
            r = slice(t * HALF, (t + 1) * HALF)
            s = mm(qx[r], keys)
            pos = (t % 2) * HALF + lax.broadcasted_iota(jnp.int32, (HALF, TOK), 0)
            s = jnp.where(lax.broadcasted_iota(jnp.int32, (HALF, TOK), 1) <= pos, s, -BIG)
            m = jnp.max(s, axis=1, keepdims=True)
            p = jnp.exp2((s - m) * SCALE).astype(BF16)
            acc[r] = mm(p, values, ABT)
            top[r] = jnp.broadcast_to(m, (HALF, DH))

    def visit(d):
        keys, values = keys_of(d), values_of(d)
        tiles = [slice(t * HALF, (t + 1) * HALF) for t in range(2 * TOK // HALF)]
        scores = mm(qx[tiles[0]], keys)
        for t, r in enumerate(tiles):
            s = scores
            if t + 1 < len(tiles):
                scores = mm(qx[tiles[t + 1]], keys)
            old = top[r]
            m = jnp.maximum(old, jnp.max(s, axis=1, keepdims=True))
            top[r] = m
            p = jnp.exp2((s - jnp.concatenate([m] * (TOK // DH), axis=1)) * SCALE).astype(BF16)
            shrink = jnp.exp2((old - m) * SCALE)
            acc[r] = jnp.concatenate([shrink, shrink], axis=1) * acc[r] + mm(p, values, ABT)

    pass_far(4 * PAIRED)
    all_aside(PAIRED, lambda shift: aside_far(shift).start())
    pass_own(2)
    arrived(0)
    diagonal()
    for d in range(3, LOOK + 1):
        pass_own(d)
    pass_far(1)

    def loop_body(d, c):
        pass_own(d + LOOK)
        pl.when(d + 1 != 4 * PAIRED)(lambda: pass_far(d + 1))
        arrived(d)
        visit(d)
        return c

    early = jnp.minimum(n_lo, ROW_AT)
    late = jnp.minimum(n_lo, COLUMN_AT)
    lax.fori_loop(1, early + 1, loop_body, 0)

    for k in range(1, 4):
        pl.when((line < 3) | (col >= k))(lambda: r_copy(k).wait_recv())
    line_first = line * 4 * TOK
    enter_row = []
    enter_factor = []
    for h in range(2):
        total = jnp.zeros((DH, DH), F32)
        before = jnp.zeros((DH, DH), F32)
        factor = jnp.ones((1, DH), F32)
        factor_before = jnp.ones((1, DH), F32)
        plain = jnp.ones((1, DH), F32)
        for x in range(4):
            block = row_st[lax.rem(col - x + 4, 4)]
            own = col == x
            before = jnp.where(own, total, before)
            factor_before = jnp.where(own, factor, factor_before)
            f = factor_of(block, h)
            fk = f * kept(line_first + x * TOK, line_first + (x + 1) * TOK - 1)
            total = fk * total + block[h * DH : (h + 1) * DH].astype(F32)
            factor = factor * fk
            plain = plain * f
        carry[h] = before
        enter_factor.append(factor_before)
        enter_row.append(plain)
        col_st[0, h * DH : (h + 1) * DH] = total.astype(BF16)
    col_st[0, 2 * DH :] = factor_rows(enter_row[0], enter_row[1])
    lax.fori_loop(1, n_down + 1, lambda k, c: (c_copy(k).start(), c)[1], 0)

    lax.fori_loop(early + 1, late + 1, loop_body, 0)

    def column(i, state):
        k = line - i
        c_copy(k).wait_recv()
        block = col_st[k]
        first = i * 4 * TOK
        keep = kept(first, first + 4 * TOK - 1)
        return tuple(
            keep * factor_of(block, h) * state[h] + block[h * DH : (h + 1) * DH].astype(F32) for h in range(2)
        )

    entered = lax.fori_loop(0, line, column, (jnp.zeros((DH, DH), F32), jnp.zeros((DH, DH), F32)))
    for h in range(2):
        state = enter_factor[h] * entered[h] + carry[h]
        for b in range(2):
            r, c, _, down_col = parts(b, h)
            first = base + b * BLK
            mine = jnp.where(doc_start(first + col_pos) <= first - 1, jnp.exp(down_col), 0.0)
            full = raw[r, c] + mine * mm(lq[r, c], state.astype(BF16))
            scale = lax.rsqrt(jnp.mean(full * full, axis=1, keepdims=True) + 1e-6)
            lin_out[r, c] = (full * scale * gain[:, c]).astype(BF16)
            if b == 0:
                state = kept(base, base + BLK - 1) * through(0, h) * state + first_up[h]

    lax.fori_loop(late + 1, n_lo + 1, loop_body, 0)

    for t in range(4):
        r = slice(t * HALF, (t + 1) * HALF)
        out = acc[r, :DH] / acc[r, DH:]
        h, b = t // 2, t % 2
        soft_out[b * HALF : (b + 1) * HALF, h * DH : (h + 1) * DH] = out.astype(BF16)

    def sent(d, c):
        s_copy(d).wait_send()
        pl.when(~far(d))(lambda: z_copy(d).wait_send())
        t_copy(d).wait_send()
        return c

    lax.fori_loop(0, n_lo + 1, sent, 0)
    lax.fori_loop(2, n_down + 1, lambda k, c: (down(k).wait_send(), c)[1], 0)
    all_near(lambda shift: near(shift).wait_send())
    pl.when(line + PAIRED <= 3)(lambda: down_far().wait_send())
    for k in (0, 2, 3):
        all_aside(k, lambda shift: aside(k, shift).wait_send())
    all_aside(PAIRED, lambda shift: aside_far(shift).wait_send())
    for k in range(1, 4):
        pl.when((line < 3) | (col + k <= 3))(lambda: r_copy(k).wait_send())
    lax.fori_loop(1, n_down + 1, lambda k, c: (c_copy(k).wait_send(), c)[1], 0)


def local(doc_lengths, lin_q, lin_k, lin_v, log_decay, lin_gain, soft_q, soft_k, soft_v):
    vmem = pltpu.VMEM
    dma = pltpu.SemaphoreType.DMA
    wide = (TOK, 2 * DH)
    slots = REACH + 1
    return pl.pallas_call(
        kernel,
        out_shape=(jax.ShapeDtypeStruct(wide, BF16), jax.ShapeDtypeStruct(wide, BF16)),
        in_specs=[pl.BlockSpec(memory_space=pltpu.SMEM)] + [pl.BlockSpec(memory_space=pl.ANY)] * 8,
        out_specs=(pl.BlockSpec(memory_space=vmem), pl.BlockSpec(memory_space=vmem)),
        scratch_shapes=[
            vmem(wide, BF16), vmem(wide, BF16), vmem(wide, BF16), vmem((2, TOK), F32), vmem((1, 2 * DH), F32),
            vmem(wide, BF16),
            vmem((slots, 4, 64, TOK), BF16), vmem((2 * TOK, 2 * DH), BF16), vmem((2 * TOK, DH), F32),
            vmem((2 * TOK, 2 * DH), F32), vmem(wide, F32), vmem((BLK, 8), F32),
            vmem((4, 2 * DH + 16, DH), BF16), vmem((4, 2 * DH + 16, DH), BF16), vmem((2, DH, DH), F32),
            vmem((2, DH, DH), F32),
            dma((8,)), dma((4,)), dma((slots,)), dma((8,)), dma((4, 7)), dma((slots,)), dma((slots,)), dma((slots,)),
            dma((slots,)), dma((slots,)), dma((slots,)), dma((4,)), dma((4,)), dma((4,)), dma((4,)),
        ],
        compiler_params=pltpu.CompilerParams(
            collective_id=0, has_side_effects=True, vmem_limit_bytes=60 * 1024 * 1024
        ),
    )(doc_lengths, lin_q, lin_k, lin_v, log_decay, lin_gain.reshape(1, 2 * DH), soft_q, soft_k.T, soft_v.T)


def solution(mesh):
    both = P("ctx", "head")
    return jax.shard_map(
        local,
        mesh=mesh,
        in_specs=(P(), both, both, both, P("head", "ctx"), P("head"), both, both, both),
        out_specs=(both, both),
        check_vma=False,
    )
```
